32 devices in a mesh: morton: 8 (over y, x, core), sub: 4 (over z).
Axes of the slice: x: 2, y: 2, z: 4, core: 2. Of those that a mesh axis runs over, the one named last changes fastest.
Arguments:
- leaf_dens: bfloat16 [512, 8, 294], P(('morton', 'sub')), may hold values from -6 to 6
- leaf_sources: int32 [512, 189], P(('morton', 'sub')), may hold values from 0 to 191, as said below
- leaf_classes: int32 [512, 189], P(('morton', 'sub')), may hold values from 0 to 15
- grand_sources: int32 [8, 189], P('morton'), may hold values from 0 to 7
- grand_classes: int32 [8, 189], P('morton'), may hold values from 0 to 15
- up_ops: bfloat16 [8, 294, 294], replicated, may hold values from -0.125 to 0.125
- far_ops: bfloat16 [16, 294, 294], replicated, may hold values from -0.02734375 to 0.02734375
- down_ops: bfloat16 [8, 294, 294], replicated, may hold values from -0.375 to 0.375
Outputs:
- leaf_local: bfloat16 [512, 8, 294], P(('morton', 'sub'))
The draws below stay inside these ranges and needn't reach their ends.
Inputs may be any that keep to these rules, and one draw needn't show every extreme that they name: `leaf_sources`: positions in the pool of the finest octants of three Morton ranges of 64 octants each (range t // 64 - 1, its own, and the next); rows of the first range never name the range before it and rows of the last never name the range after it.
All inputs are finite; a program needn't handle non-finite values.
Results may differ from the reference program's by a relative error of at most 0.0085.
Values may be sent and summed in bfloat16 or wider, within the bound.
No kernel may reach another device: no remote copies, remote signals or barrier semaphores. Data moves between devices by JAX's collectives and lax.ppermute only.
A program may use at most 64 MiB of HBM per device.

```python
import jax
import jax.numpy as jnp
from jax import lax

W = 294
VL = 189
CLASSES = 16
NRHS = 8
LEAVES = 512
PARENTS = 64
GRANDS = 8
GROUP = 64


def draw_leaf_sources(key, part):
    row_index = jnp.arange(LEAVES, dtype=jnp.int32)
    range_index = row_index // GROUP
    last_range = LEAVES // GROUP - 1
    lower_bound = jnp.where(range_index > 0, 0, GROUP).astype(jnp.int32)
    upper_bound = jnp.where(range_index < last_range, 3 * GROUP, 2 * GROUP).astype(jnp.int32)
    return jax.random.randint(jax.random.fold_in(key, 11), (LEAVES, VL), lower_bound[:, None], upper_bound[:, None], dtype=jnp.int32)


def place_ends(result, stream_key, low, top_value):
    spot = [jax.random.randint(jax.random.fold_in(stream_key, axis), (), 0, length) for axis, length in enumerate(result.shape)]
    widest = result.shape.index(max(result.shape))
    beside = spot[:widest] + [(spot[widest] + 1) % result.shape[widest]] + spot[widest + 1:]
    return result.at[tuple(spot)].set(low).at[tuple(beside)].set(top_value)


def block_scale(rng, dims, split, least, high):
    loudness, own = 1.0, jax.random.fold_in(rng, 6)
    for dim, shards_of in split:
        draws = jnp.exp(jax.random.uniform(jax.random.fold_in(own, dim), (shards_of,), jnp.float32, least / len(split), high / len(split)))
        loudness = loudness * jnp.repeat(draws, dims[dim] // shards_of).reshape([-1 if axis == dim else 1 for axis in range(len(dims))])
    return loudness


def noise(own_key, shape, width, bound, cuts=(), kind=jnp.bfloat16):
    factor_of = block_scale(own_key, shape, cuts, -0.22, 0.18) if cuts else 1.0
    result = jax.random.normal(own_key, shape, jnp.float32) * width * factor_of
    return jnp.minimum(jnp.maximum(result, -bound), bound).astype(kind)


def setup_inputs(seed: int = 0) -> dict:
    keys = jax.random.split(jax.random.key(seed), 9)
    leaf_dens = noise(keys[0], (LEAVES, NRHS, W), 1.0, 6.0, ((0, 32),))
    leaf_sources = draw_leaf_sources(jax.random.fold_in(keys[8], 71), 0)
    leaf_classes = place_ends(jax.random.randint(keys[2], (LEAVES, VL), 0, CLASSES), jax.random.fold_in(keys[2], 1), 0, CLASSES - 1).astype(jnp.int32)
    grand_sources = place_ends(jax.random.randint(keys[3], (GRANDS, VL), 0, GRANDS), jax.random.fold_in(keys[3], 1), 0, GRANDS - 1).astype(jnp.int32)
    grand_classes = place_ends(jax.random.randint(keys[4], (GRANDS, VL), 0, CLASSES), jax.random.fold_in(keys[4], 1), 0, CLASSES - 1).astype(jnp.int32)
    up_ops = noise(keys[5], (8, W, W), (8 * W) ** -0.5, 0.125)
    far_ops = noise(keys[6], (CLASSES, W, W), (VL * W) ** -0.5, 0.02734375)
    down_ops = noise(keys[7], (8, W, W), W ** -0.5, 0.375)
    return dict(leaf_dens=leaf_dens, leaf_sources=leaf_sources, leaf_classes=leaf_classes, grand_sources=grand_sources, grand_classes=grand_classes, up_ops=up_ops, far_ops=far_ops, down_ops=down_ops)


def widen(array):
    return array.astype(jnp.float32)


def rounded(array):
    return widen(lax.optimization_barrier(array.astype(jnp.bfloat16)))


def far_sums(pool, sources, classes):
    targets = sources.shape[0]
    segment_ids = (jnp.arange(targets, dtype=jnp.int32)[:, None] * CLASSES + classes).reshape(-1)
    taken = pool[sources.reshape(-1)]
    return jax.ops.segment_sum(taken, segment_ids, num_segments=targets * CLASSES)


def reference(leaf_dens, leaf_sources, leaf_classes, grand_sources, grand_classes, up_ops, far_ops, down_ops):
    width_all = NRHS * W
    up_wide = widen(up_ops)
    down_wide = widen(down_ops)
    far_wide = widen(far_ops).reshape(CLASSES * W, W)
    children = widen(leaf_dens).reshape(PARENTS, 8, NRHS, W)
    parent_dens = rounded(jnp.einsum("pknw,kwv->pnv", children, up_wide))
    grand_dens = rounded(jnp.einsum("gknw,kwv->gnv", parent_dens.reshape(GRANDS, 8, NRHS, W), up_wide))

    def translate(aggregate, targets):
        rows_in = rounded(aggregate).reshape(targets, CLASSES, NRHS, W).transpose(0, 2, 1, 3)
        rows_in = rows_in.reshape(targets * NRHS, CLASSES * W)
        return jnp.dot(rows_in, far_wide, precision=lax.Precision.HIGHEST).reshape(targets, NRHS, W)

    grand_agg = far_sums(grand_dens.reshape(GRANDS, width_all), grand_sources, grand_classes)
    grand_local = rounded(translate(grand_agg, GRANDS))
    parent_local = rounded(jnp.einsum("gnw,kwv->gknv", grand_local, down_wide).reshape(PARENTS, NRHS, W))
    ranges = LEAVES // GROUP
    leaf_wide = widen(leaf_dens).reshape(ranges, GROUP, width_all)
    empty = jnp.zeros((1, GROUP, width_all), jnp.float32)
    padded = jnp.concatenate([empty, leaf_wide, empty], axis=0)

    def one_range(index):
        pool = lax.dynamic_slice_in_dim(padded, index, 3, 0).reshape(3 * GROUP, width_all)
        sources = lax.dynamic_slice_in_dim(leaf_sources, index * GROUP, GROUP, 0)
        classes = lax.dynamic_slice_in_dim(leaf_classes, index * GROUP, GROUP, 0)
        return translate(far_sums(pool, sources, classes), GROUP)

    leaf_far = lax.map(one_range, jnp.arange(ranges, dtype=jnp.int32)).reshape(LEAVES, NRHS, W)
    downward = jnp.einsum("pnw,kwv->pknv", parent_local, down_wide).reshape(LEAVES, NRHS, W)
    return (leaf_far + downward).astype(jnp.bfloat16)
```

```python
import jax
import jax.numpy as jnp
from jax import lax
from jax.sharding import PartitionSpec as P


def swapped(value, axis, mask):
    count = lax.axis_size(axis)
    return lax.ppermute(value, axis, [(i, i ^ mask) for i in range(count)])


def doubled(rows, axis, masks):
    own = rows.shape[0]
    pieces = {0: 0}
    for mask in masks:
        other = swapped(rows, axis, mask)
        pieces.update({p ^ mask: at + len(pieces) for p, at in list(pieces.items())})
        rows = jnp.concatenate([rows, other], axis=0)
    return jnp.concatenate(
        [rows[pieces[p] * own : (pieces[p] + 1) * own] for p in range(len(pieces))], axis=0
    )


def bits_down(count):
    return [1 << bit for bit in reversed(range(count.bit_length() - 1))]


def unxored(rows, index, count):
    for bit in range(count.bit_length() - 1):
        shape = rows.shape
        split = rows.reshape((count >> (bit + 1), 2, 1 << bit) + shape[1:])
        flipped = jnp.concatenate([split[:, 1:], split[:, :1]], axis=1)
        rows = jnp.where((index >> bit) % 2 == 1, flipped, split).reshape(shape)
    return rows


def class_counts(sources, classes, pool_size, classes_count):
    source_hot = (
        sources[:, :, None] == jnp.arange(pool_size, dtype=jnp.int32)[None, None, :]
    ).astype(jnp.bfloat16)
    class_hot = (
        classes[:, :, None] == jnp.arange(classes_count, dtype=jnp.int32)[None, None, :]
    ).astype(jnp.bfloat16)
    return jnp.einsum(
        "tec,teq->tcq", class_hot, source_hot, preferred_element_type=jnp.float32
    ).astype(jnp.bfloat16)


def shards(
    leaf_dens, leaf_sources, leaf_classes, grand_sources, grand_classes, up_ops, far_ops, down_ops
):
    own_leaves, rhs_count, width = leaf_dens.shape
    classes_count = far_ops.shape[0]
    sub_count = lax.axis_size("sub")
    morton_count = lax.axis_size("morton")
    sub_index = lax.axis_index("sub")
    morton_index = lax.axis_index("morton")
    range_size = own_leaves * sub_count
    flat_width = rhs_count * width
    grand_span = 64 // own_leaves
    grands_here = range_size // 64
    position = sub_index % grand_span
    parents_here = own_leaves // 8
    far_matrix = far_ops.reshape(classes_count * width, width)

    own = leaf_dens.reshape(own_leaves, flat_width)
    range_rows = doubled(own, "sub", bits_down(sub_count))
    outer = [(i, i + 1) for i in range(1, morton_count - 1, 2)]
    outer = outer + [(j, i) for i, j in outer]
    outer_rows = lax.ppermute(range_rows, "morton", outer)
    inner_rows = swapped(range_rows, "morton", 1)

    children = range_rows.reshape(range_size // 8, 8, rhs_count, width)
    parent_dens = jnp.einsum(
        "jknw,kwv->jnv", children, up_ops, preferred_element_type=jnp.float32
    ).astype(jnp.bfloat16)
    parent_dens = parent_dens.reshape(grands_here, grand_span, parents_here, rhs_count, width)
    parent_dens = unxored(parent_dens.transpose(1, 0, 2, 3, 4), position, grand_span)
    parent_dens = parent_dens.transpose(1, 0, 2, 3, 4).reshape(grands_here, 8, rhs_count, width)
    grand_dens = jnp.einsum(
        "gknw,kwv->gnv", parent_dens, up_ops, preferred_element_type=jnp.float32
    ).astype(jnp.bfloat16)
    grand_pool = doubled(
        grand_dens.reshape(grands_here, flat_width),
        "morton",
        list(reversed(bits_down(morton_count))),
    )
    grand_count = grand_pool.shape[0]
    row_pick = sub_index // grand_span
    my_sources = lax.dynamic_slice_in_dim(grand_sources, row_pick, 1, 0)
    my_classes = lax.dynamic_slice_in_dim(grand_classes, row_pick, 1, 0)
    my_sources = my_sources ^ (morton_index * grands_here + row_pick)
    grand_counts = class_counts(my_sources, my_classes, grand_count, classes_count)[0]
    grand_agg = jnp.dot(grand_counts, grand_pool, preferred_element_type=jnp.float32).astype(
        jnp.bfloat16
    )

    slot = leaf_sources // range_size
    slot = jnp.where(morton_index % 2 == 1, slot, 2 - slot)
    places = slot * range_size + ((leaf_sources % range_size) ^ (sub_index * own_leaves))
    counts = class_counts(places, leaf_classes, 3 * range_size, classes_count)
    pool_rows = jnp.concatenate([inner_rows, range_rows, outer_rows], axis=0)
    aggregate = jnp.dot(
        counts.reshape(own_leaves * classes_count, 3 * range_size),
        pool_rows,
        preferred_element_type=jnp.float32,
    ).astype(jnp.bfloat16)
    aggregate = jnp.concatenate([aggregate, grand_agg], axis=0)
    rows_in = aggregate.reshape(own_leaves + 1, classes_count, rhs_count, width)
    rows_in = rows_in.transpose(0, 2, 1, 3).reshape(
        (own_leaves + 1) * rhs_count, classes_count * width
    )
    far = jnp.dot(rows_in, far_matrix, preferred_element_type=jnp.float32)
    far = far.reshape(own_leaves + 1, rhs_count, width)
    leaf_far, grand_local = far[:-1], far[-1].astype(jnp.bfloat16)

    parent_ops = lax.dynamic_slice_in_dim(down_ops, position * parents_here, parents_here, 0)
    parent_local = jnp.einsum(
        "nw,jwv->jnv", grand_local, parent_ops, preferred_element_type=jnp.float32
    ).astype(jnp.bfloat16)
    downward = jnp.einsum(
        "jnw,kwv->jknv", parent_local, down_ops, preferred_element_type=jnp.float32
    )
    downward = downward.reshape(own_leaves, rhs_count, width)
    return (leaf_far + downward).astype(jnp.bfloat16)


def solution(mesh):
    placed = (
        P(("morton", "sub"), None, None),
        P(("morton", "sub"), None),
        P(("morton", "sub"), None),
        P("morton", None),
        P("morton", None),
        P(),
        P(),
        P(),
    )
    return jax.shard_map(
        shards,
        mesh=mesh,
        in_specs=placed,
        out_specs=P(("morton", "sub"), None, None),
        check_vma=False,
    )
```

```python
import functools

import jax
import jax.numpy as jnp
from jax import lax
from jax.experimental import pallas as pl
from jax.experimental.pallas import tpu as pltpu
from jax.sharding import PartitionSpec as P

LANES = 128
F32 = jnp.float32
BF16 = jnp.bfloat16


def swapped(value, axis, mask):
    count = lax.axis_size(axis)
    return lax.ppermute(value, axis, [(i, i ^ mask) for i in range(count)])


def masks_of(count):
    return [1 << bit for bit in range(count.bit_length() - 1)]


class Lanes:
    def __init__(self, rhs_count, width):
        self.rhs_count, self.width = rhs_count, width
        self.main = width // LANES * LANES
        self.tail = width - self.main
        self.per_tile = LANES // self.tail if self.tail else 1
        self.tail_tiles = -(-rhs_count // self.per_tile) if self.tail else 0
        self.total = rhs_count * self.main + self.tail_tiles * LANES

    def main_of(self, n):
        return slice(n * self.main, (n + 1) * self.main)

    def tail_of(self, n):
        start = self.rhs_count * self.main + n // self.per_tile * LANES
        start += n % self.per_tile * self.tail
        return slice(start, start + self.tail)

    def take(self, rows, n):
        return jnp.concatenate([rows[:, self.main_of(n)], rows[:, self.tail_of(n)]], axis=1)


def tiles_of(width):
    return -(-width // LANES)


def fill(scratch, rows):
    for tile in range(scratch.shape[0]):
        part = rows[:, tile * LANES : (tile + 1) * LANES]
        scratch[tile, :, : part.shape[1]] = part


def every(scratch, start, size, stride, width):
    parts = [scratch[tile, pl.ds(start, size, stride=stride), :] for tile in range(tiles_of(width))]
    parts[-1] = parts[-1][:, : width - (len(parts) - 1) * LANES]
    return jnp.concatenate(parts, axis=1)


def flat_kernel(lanes, dens_ref, out_ref, wide):
    own, rhs_count, width = dens_ref.shape
    fill(wide, dens_ref[...].astype(F32).reshape(own * rhs_count, width))
    tails = []
    for n in range(rhs_count):
        rows = every(wide, n, own, rhs_count, width).astype(BF16)
        out_ref[:, lanes.main_of(n)] = rows[:, : lanes.main]
        tails.append(rows[:, lanes.main :])
    for tile in range(lanes.tail_tiles):
        parts = tails[tile * lanes.per_tile : (tile + 1) * lanes.per_tile]
        spare = LANES - len(parts) * lanes.tail
        parts.append(jnp.zeros((own, spare), BF16))
        start = rhs_count * lanes.main + tile * LANES
        out_ref[:, start : start + LANES] = jnp.concatenate(parts, axis=1)


def hot_rows(values, count):
    rows = lax.broadcasted_iota(jnp.int32, (count, values.shape[1]), 0)
    return jnp.where(rows == values, 1.0, 0.0).astype(BF16)


def class_counts(classes, sources, classes_count, pool_size):
    return lax.dot_general(
        hot_rows(classes, classes_count),
        hot_rows(sources, pool_size),
        (((1,), (1,)), ((), ())),
        preferred_element_type=F32,
    )


def counts_kernel(
    rhs_count,
    index_ref,
    sources_ref,
    classes_ref,
    grand_sources_ref,
    grand_classes_ref,
    counts_ref,
    grand_counts_ref,
    wide,
):
    own = sources_ref.shape[0]
    pool_size = counts_ref.shape[1]
    classes_count = counts_ref.shape[0] // own
    range_size = pool_size // 3
    sub_index, odd, row_pick, grand_index = (index_ref[i] for i in range(4))
    for t in range(own):
        sources = sources_ref[t : t + 1, :]
        slot = sources // range_size
        inside = sources - slot * range_size
        slot = jnp.where(odd == 1, slot, 2 - slot)
        places = slot * range_size + (inside ^ (sub_index * own))
        counts = class_counts(
            classes_ref[t : t + 1, :], places, classes_count, wide.shape[0] * LANES
        )
        for tile in range(wide.shape[0]):
            part = counts[:, tile * LANES : (tile + 1) * LANES]
            wide[tile, pl.ds(t, classes_count, stride=own), :] = part
    counts_ref[...] = every(wide, 0, own * classes_count, 1, pool_size).astype(BF16)
    group = grand_counts_ref.shape[0] // classes_count
    spread = grand_counts_ref.shape[1]
    places = grand_sources_ref[pl.ds(row_pick, 1), :] ^ grand_index
    classes = grand_classes_ref[pl.ds(row_pick, 1), :]
    entries = places.shape[1]
    column_grand = lax.broadcasted_iota(jnp.int32, (spread, entries), 0) // rhs_count
    source_hot = jnp.where(column_grand == places, 1.0, 0.0).astype(BF16)
    row_class = lax.broadcasted_iota(jnp.int32, (classes_count * group, entries), 0) // group
    class_hot = jnp.where(row_class == classes, 1.0, 0.0).astype(BF16)
    all_pairs = lax.dot_general(
        class_hot, source_hot, (((1,), (1,)), ((), ())), preferred_element_type=F32
    )
    row_rhs = lax.broadcasted_iota(jnp.int32, all_pairs.shape, 0) % group
    column_rhs = lax.broadcasted_iota(jnp.int32, all_pairs.shape, 1) % rhs_count
    grand_counts_ref[...] = jnp.where(row_rhs == column_rhs, all_pairs, 0.0).astype(BF16)


def grand_kernel(lanes, span, index_ref, rows_ref, up_ref, out_ref, wide, parents):
    rhs_count, width = lanes.rhs_count, lanes.width
    range_size = rows_ref.shape[0]
    fan = up_ref.shape[0]
    parent_count = range_size // fan
    position = index_ref[0]
    fill(wide, rows_ref[...].astype(F32))
    total = jnp.zeros((rhs_count * parent_count, width), F32)
    for k in range(fan):
        rows = every(wide, k, parent_count, fan, lanes.total)
        left = jnp.concatenate([lanes.take(rows, n) for n in range(rhs_count)], axis=0)
        total += jnp.dot(left.astype(BF16), up_ref[k], preferred_element_type=F32)
    fill(parents, total.astype(BF16).astype(F32))
    per_block = fan // span
    for grand in range(parent_count // fan):
        total = jnp.zeros((rhs_count, width), F32)
        for child in range(fan):
            rows = every(parents, grand * fan + child, rhs_count, parent_count, width)
            operator = ((child // per_block) ^ position) * per_block + child % per_block
            total += jnp.dot(rows.astype(BF16), up_ref[operator], preferred_element_type=F32)
        out_ref[grand * rhs_count : (grand + 1) * rhs_count, :] = total.astype(BF16)


def far_kernel(
    lanes,
    index_ref,
    counts_ref,
    grand_counts_ref,
    inner_ref,
    range_ref,
    outer_ref,
    grand_pool_ref,
    far_ref,
    down_ref,
    out_ref,
    aggregate,
    grand_aggregate,
    far_rows,
):
    own, rhs_count, width = out_ref.shape
    classes_count = far_ref.shape[0]
    fan = down_ref.shape[0]
    group = grand_counts_ref.shape[0] // classes_count
    parents_here = own // fan
    position = index_ref[0]
    grand_aggregate[...] = jnp.dot(
        grand_counts_ref[...], grand_pool_ref[...], preferred_element_type=F32
    ).astype(BF16)
    pool = jnp.concatenate([inner_ref[...], range_ref[...], outer_ref[...]], axis=0)
    aggregate[...] = jnp.dot(counts_ref[...], pool, preferred_element_type=F32).astype(BF16)
    total = jnp.zeros((rhs_count * own + group, width), F32)
    for c in range(classes_count):
        rows = aggregate[c * own : (c + 1) * own, :]
        parts = [lanes.take(rows, n) for n in range(rhs_count)]
        parts.append(grand_aggregate[c * group : (c + 1) * group, :])
        total += jnp.dot(jnp.concatenate(parts, axis=0), far_ref[c], preferred_element_type=F32)
    pad = jnp.zeros((own, far_rows.shape[0] * LANES - width), F32)
    for n in range(rhs_count):
        rows = jnp.concatenate([total[n * own : (n + 1) * own, :], pad], axis=1)
        for tile in range(far_rows.shape[0]):
            part = rows[:, tile * LANES : (tile + 1) * LANES]
            far_rows[tile, pl.ds(n, own, stride=rhs_count), :] = part
    grand_local = total[rhs_count * own :, :].astype(BF16)
    parent_local = []
    for j in range(parents_here):
        operator = down_ref[position * parents_here + j]
        local = jnp.dot(grand_local, operator, preferred_element_type=F32)
        parent_local.append(local[:rhs_count, :])
    parent_local = jnp.concatenate(parent_local, axis=0).astype(BF16)
    for k in range(fan):
        downward = jnp.dot(parent_local, down_ref[k], preferred_element_type=F32)
        for j in range(parents_here):
            leaf = j * fan + k
            local = every(far_rows, leaf * rhs_count, rhs_count, 1, width)
            local += downward[j * rhs_count : (j + 1) * rhs_count, :]
            out_ref[leaf] = local.astype(BF16)


def tiled(rows, width):
    return pltpu.VMEM((tiles_of(width), rows, LANES), F32)


def call(kernel, outs, scratch, scalars, *operands):
    whole = pl.BlockSpec(memory_space=pltpu.VMEM)
    specs = [pl.BlockSpec(memory_space=pltpu.SMEM)] * len(scalars) + [whole] * len(operands)
    return pl.pallas_call(
        kernel,
        out_shape=outs,
        in_specs=specs,
        out_specs=jax.tree.map(lambda _: whole, outs),
        scratch_shapes=scratch,
    )(*scalars, *operands)


def shards(
    leaf_dens, leaf_sources, leaf_classes, grand_sources, grand_classes, up_ops, far_ops, down_ops
):
    own, rhs_count, width = leaf_dens.shape
    classes_count = far_ops.shape[0]
    fan = up_ops.shape[0]
    sub_count, morton_count = lax.axis_size("sub"), lax.axis_size("morton")
    sub_index, morton_index = lax.axis_index("sub"), lax.axis_index("morton")
    range_size = own * sub_count
    leaves_of_grand = fan * fan
    grand_span = leaves_of_grand // own
    grands_here = range_size // leaves_of_grand
    grand_count = morton_count * grands_here
    position = sub_index % grand_span
    row_pick = sub_index // grand_span
    lanes = Lanes(rhs_count, width)
    struct = jax.ShapeDtypeStruct

    rows = call(
        functools.partial(flat_kernel, lanes),
        struct((own, lanes.total), BF16),
        [tiled(own * rhs_count, width)],
        [],
        leaf_dens,
    )
    blocks = {0: rows}
    for mask in reversed(masks_of(sub_count)):
        held = sorted(blocks)
        joined = jnp.concatenate([blocks[p] for p in held], axis=0) if len(held) > 1 else rows
        other = swapped(joined, "sub", mask)
        for at, p in enumerate(held):
            blocks[p ^ mask] = other[at * own : (at + 1) * own]
    range_rows = jnp.concatenate([blocks[p] for p in range(sub_count)], axis=0)
    outer = [(i, i + 1) for i in range(1, morton_count - 1, 2)]
    outer = outer + [(j, i) for i, j in outer]
    outer_rows = lax.ppermute(range_rows, "morton", outer)
    inner_rows = swapped(range_rows, "morton", 1)

    index = jnp.stack(
        [sub_index, morton_index % 2, row_pick, morton_index * grands_here + row_pick]
    ).astype(jnp.int32)
    group = -(-rhs_count // 16) * 16
    counts, grand_counts = call(
        functools.partial(counts_kernel, rhs_count),
        (
            struct((classes_count * own, 3 * range_size), BF16),
            struct((classes_count * group, grand_count * rhs_count), BF16),
        ),
        [tiled(classes_count * own, 3 * range_size)],
        [index],
        leaf_sources,
        leaf_classes,
        grand_sources,
        grand_classes,
    )

    place = position.reshape(1).astype(jnp.int32)
    grand_pool = call(
        functools.partial(grand_kernel, lanes, grand_span),
        struct((grands_here * rhs_count, width), BF16),
        [
            tiled(range_size, lanes.total),
            tiled(rhs_count * range_size // fan, width),
        ],
        [place],
        range_rows,
        up_ops,
    )
    for mask in masks_of(morton_count):
        grand_pool = jnp.concatenate([grand_pool, swapped(grand_pool, "morton", mask)], axis=0)

    return call(
        functools.partial(far_kernel, lanes),
        struct(leaf_dens.shape, BF16),
        [
            pltpu.VMEM((classes_count * own, lanes.total), BF16),
            pltpu.VMEM((classes_count * group, width), BF16),
            tiled(own * rhs_count, width),
        ],
        [place],
        counts,
        grand_counts,
        inner_rows,
        range_rows,
        outer_rows,
        grand_pool,
        far_ops,
        down_ops,
    )


def solution(mesh):
    placed = (
        P(("morton", "sub"), None, None),
        P(("morton", "sub"), None),
        P(("morton", "sub"), None),
        P("morton", None),
        P("morton", None),
        P(),
        P(),
        P(),
    )
    return jax.shard_map(
        shards,
        mesh=mesh,
        in_specs=placed,
        out_specs=P(("morton", "sub"), None, None),
        check_vma=False,
    )
```

```python
import functools

import jax
import jax.numpy as jnp
from jax import lax
from jax.experimental import pallas as pl
from jax.experimental.pallas import tpu as pltpu
from jax.sharding import PartitionSpec as P

LANES = 128
F32 = jnp.float32
BF16 = jnp.bfloat16


def swapped(value, axis, mask):
    count = lax.axis_size(axis)
    return lax.ppermute(value, axis, [(i, i ^ mask) for i in range(count)])


def masks_of(count):
    return [1 << bit for bit in range(count.bit_length() - 1)]


class Lanes:
    def __init__(self, rhs_count, width):
        self.rhs_count, self.width = rhs_count, width
        self.main = width // LANES * LANES
        self.tail = width - self.main
        self.per_tile = LANES // self.tail if self.tail else 1
        self.tail_tiles = -(-rhs_count // self.per_tile) if self.tail else 0
        self.total = rhs_count * self.main + self.tail_tiles * LANES

    def main_of(self, n):
        return slice(n * self.main, (n + 1) * self.main)

    def tail_of(self, n):
        start = self.rhs_count * self.main + n // self.per_tile * LANES
        start += n % self.per_tile * self.tail
        return slice(start, start + self.tail)

    def take(self, rows, n):
        return jnp.concatenate([rows[:, self.main_of(n)], rows[:, self.tail_of(n)]], axis=1)


def tiles_of(width):
    return -(-width // LANES)


def fill(scratch, rows):
    for tile in range(scratch.shape[0]):
        part = rows[:, tile * LANES : (tile + 1) * LANES]
        scratch[tile, :, : part.shape[1]] = part


def every(scratch, start, size, stride, width):
    parts = [scratch[tile, pl.ds(start, size, stride=stride), :] for tile in range(tiles_of(width))]
    parts[-1] = parts[-1][:, : width - (len(parts) - 1) * LANES]
    return jnp.concatenate(parts, axis=1)


def flat_kernel(lanes, dens_ref, out_ref, wide):
    own, rhs_count, width = dens_ref.shape
    fill(wide, dens_ref[...].astype(F32).reshape(own * rhs_count, width))
    tails = []
    for n in range(rhs_count):
        rows = every(wide, n, own, rhs_count, width).astype(BF16)
        out_ref[:, lanes.main_of(n)] = rows[:, : lanes.main]
        tails.append(rows[:, lanes.main :])
    for tile in range(lanes.tail_tiles):
        parts = tails[tile * lanes.per_tile : (tile + 1) * lanes.per_tile]
        spare = LANES - len(parts) * lanes.tail
        parts.append(jnp.zeros((own, spare), BF16))
        start = rhs_count * lanes.main + tile * LANES
        out_ref[:, start : start + LANES] = jnp.concatenate(parts, axis=1)


def hot_rows(values, count):
    rows = lax.broadcasted_iota(jnp.int32, (count, values.shape[1]), 0)
    return jnp.where(rows == values, 1.0, 0.0).astype(BF16)


def class_counts(classes, sources, classes_count, pool_size):
    return lax.dot_general(
        hot_rows(classes, classes_count),
        hot_rows(sources, pool_size),
        (((1,), (1,)), ((), ())),
        preferred_element_type=F32,
    )


def counts_kernel(
    rhs_count,
    span,
    sources_ref,
    classes_ref,
    grand_sources_ref,
    grand_classes_ref,
    counts_ref,
    grand_counts_ref,
    wide,
):
    own = sources_ref.shape[0]
    pool_size = counts_ref.shape[1]
    classes_count = counts_ref.shape[0] // own
    range_size = pool_size // 3
    sub_index, morton_index = lax.axis_index("sub"), lax.axis_index("morton")
    odd = morton_index % 2
    row_pick = sub_index // span
    grand_index = morton_index * grand_sources_ref.shape[0] + row_pick
    for t in range(own):
        sources = sources_ref[t : t + 1, :]
        slot = sources // range_size
        inside = sources - slot * range_size
        slot = jnp.where(odd == 1, slot, 2 - slot)
        places = slot * range_size + (inside ^ (sub_index * own))
        counts = class_counts(
            classes_ref[t : t + 1, :], places, classes_count, wide.shape[0] * LANES
        )
        for tile in range(wide.shape[0]):
            part = counts[:, tile * LANES : (tile + 1) * LANES]
            wide[tile, pl.ds(t, classes_count, stride=own), :] = part
    counts_ref[...] = every(wide, 0, own * classes_count, 1, pool_size).astype(BF16)
    group = grand_counts_ref.shape[0] // classes_count
    spread = grand_counts_ref.shape[1]
    places = grand_sources_ref[pl.ds(row_pick, 1), :] ^ grand_index
    classes = grand_classes_ref[pl.ds(row_pick, 1), :]
    entries = places.shape[1]
    column_grand = lax.broadcasted_iota(jnp.int32, (spread, entries), 0) // rhs_count
    source_hot = jnp.where(column_grand == places, 1.0, 0.0).astype(BF16)
    row_class = lax.broadcasted_iota(jnp.int32, (classes_count * group, entries), 0) // group
    class_hot = jnp.where(row_class == classes, 1.0, 0.0).astype(BF16)
    all_pairs = lax.dot_general(
        class_hot, source_hot, (((1,), (1,)), ((), ())), preferred_element_type=F32
    )
    row_rhs = lax.broadcasted_iota(jnp.int32, all_pairs.shape, 0) % group
    column_rhs = lax.broadcasted_iota(jnp.int32, all_pairs.shape, 1) % rhs_count
    grand_counts_ref[...] = jnp.where(row_rhs == column_rhs, all_pairs, 0.0).astype(BF16)


def grand_kernel(lanes, span, rows_ref, up_ref, out_ref, wide, parents):
    rhs_count, width = lanes.rhs_count, lanes.width
    range_size = rows_ref.shape[0]
    fan = up_ref.shape[0]
    parent_count = range_size // fan
    position = lax.axis_index("sub") % span
    fill(wide, rows_ref[...].astype(F32))
    total = jnp.zeros((rhs_count * parent_count, width), F32)
    for k in range(fan):
        rows = every(wide, k, parent_count, fan, lanes.total)
        left = jnp.concatenate([lanes.take(rows, n) for n in range(rhs_count)], axis=0)
        total += jnp.dot(left.astype(BF16), up_ref[k], preferred_element_type=F32)
    fill(parents, total.astype(BF16).astype(F32))
    per_block = fan // span
    for grand in range(parent_count // fan):
        total = jnp.zeros((rhs_count, width), F32)
        for child in range(fan):
            rows = every(parents, grand * fan + child, rhs_count, parent_count, width)
            operator = ((child // per_block) ^ position) * per_block + child % per_block
            total += jnp.dot(rows.astype(BF16), up_ref[operator], preferred_element_type=F32)
        out_ref[grand * rhs_count : (grand + 1) * rhs_count, :] = total.astype(BF16)


def far_kernel(
    lanes,
    span,
    counts_ref,
    grand_counts_ref,
    inner_ref,
    range_ref,
    outer_ref,
    grand_pool_ref,
    far_ref,
    down_ref,
    out_ref,
    aggregate,
    grand_aggregate,
    far_rows,
):
    own, rhs_count, width = out_ref.shape
    classes_count = far_ref.shape[0]
    fan = down_ref.shape[0]
    group = grand_counts_ref.shape[0] // classes_count
    parents_here = own // fan
    position = lax.axis_index("sub") % span
    grand_aggregate[...] = jnp.dot(
        grand_counts_ref[...], grand_pool_ref[...], preferred_element_type=F32
    ).astype(BF16)
    pool = jnp.concatenate([inner_ref[...], range_ref[...], outer_ref[...]], axis=0)
    aggregate[...] = jnp.dot(counts_ref[...], pool, preferred_element_type=F32).astype(BF16)
    total = jnp.zeros((rhs_count * own + group, width), F32)
    for c in range(classes_count):
        rows = aggregate[c * own : (c + 1) * own, :]
        parts = [lanes.take(rows, n) for n in range(rhs_count)]
        parts.append(grand_aggregate[c * group : (c + 1) * group, :])
        total += jnp.dot(jnp.concatenate(parts, axis=0), far_ref[c], preferred_element_type=F32)
    pad = jnp.zeros((own, far_rows.shape[0] * LANES - width), F32)
    for n in range(rhs_count):
        rows = jnp.concatenate([total[n * own : (n + 1) * own, :], pad], axis=1)
        for tile in range(far_rows.shape[0]):
            part = rows[:, tile * LANES : (tile + 1) * LANES]
            far_rows[tile, pl.ds(n, own, stride=rhs_count), :] = part
    grand_local = total[rhs_count * own :, :].astype(BF16)
    parent_local = []
    for j in range(parents_here):
        operator = down_ref[position * parents_here + j]
        local = jnp.dot(grand_local, operator, preferred_element_type=F32)
        parent_local.append(local[:rhs_count, :])
    parent_local = jnp.concatenate(parent_local, axis=0).astype(BF16)
    for k in range(fan):
        downward = jnp.dot(parent_local, down_ref[k], preferred_element_type=F32)
        for j in range(parents_here):
            leaf = j * fan + k
            local = every(far_rows, leaf * rhs_count, rhs_count, 1, width)
            local += downward[j * rhs_count : (j + 1) * rhs_count, :]
            out_ref[leaf] = local.astype(BF16)


def tiled(rows, width):
    return pltpu.VMEM((tiles_of(width), rows, LANES), F32)


def call(name, kernel, outs, scratch, *operands):
    whole = pl.BlockSpec(memory_space=pltpu.VMEM)
    operands = [pltpu.with_memory_space_constraint(x, pltpu.VMEM) for x in operands]
    return pl.pallas_call(
        kernel,
        out_shape=outs,
        in_specs=[whole] * len(operands),
        out_specs=jax.tree.map(lambda _: whole, outs),
        scratch_shapes=scratch,
        compiler_params=pltpu.CompilerParams(vmem_limit_bytes=16 << 20),
        name=name,
    )(*operands)


def shards(
    leaf_dens, leaf_sources, leaf_classes, grand_sources, grand_classes, up_ops, far_ops, down_ops
):
    own, rhs_count, width = leaf_dens.shape
    classes_count = far_ops.shape[0]
    fan = up_ops.shape[0]
    sub_count, morton_count = lax.axis_size("sub"), lax.axis_size("morton")
    range_size = own * sub_count
    leaves_of_grand = fan * fan
    grand_span = leaves_of_grand // own
    grands_here = range_size // leaves_of_grand
    grand_count = morton_count * grands_here
    lanes = Lanes(rhs_count, width)
    struct = pltpu.VMEM

    rows = call(
        "flatten",
        functools.partial(flat_kernel, lanes),
        struct((own, lanes.total), BF16),
        [tiled(own * rhs_count, width)],
        leaf_dens,
    )
    blocks = {0: rows}
    for mask in reversed(masks_of(sub_count)):
        held = sorted(blocks)
        joined = jnp.concatenate([blocks[p] for p in held], axis=0) if len(held) > 1 else rows
        other = swapped(joined, "sub", mask)
        for at, p in enumerate(held):
            blocks[p ^ mask] = other[at * own : (at + 1) * own]
    range_rows = jnp.concatenate([blocks[p] for p in range(sub_count)], axis=0)
    outer = [(i, i + 1) for i in range(1, morton_count - 1, 2)]
    outer = outer + [(j, i) for i, j in outer]
    outer_rows = lax.ppermute(range_rows, "morton", outer)
    inner_rows = swapped(range_rows, "morton", 1)

    group = -(-rhs_count // 16) * 16
    counts, grand_counts = call(
        "counts",
        functools.partial(counts_kernel, rhs_count, grand_span),
        (
            struct((classes_count * own, 3 * range_size), BF16),
            struct((classes_count * group, grand_count * rhs_count), BF16),
        ),
        [tiled(classes_count * own, 3 * range_size)],
        leaf_sources,
        leaf_classes,
        grand_sources,
        grand_classes,
    )

    grand_pool = call(
        "grands",
        functools.partial(grand_kernel, lanes, grand_span),
        struct((grands_here * rhs_count, width), BF16),
        [
            tiled(range_size, lanes.total),
            tiled(rhs_count * range_size // fan, width),
        ],
        range_rows,
        up_ops,
    )
    for mask in masks_of(morton_count):
        grand_pool = jnp.concatenate([grand_pool, swapped(grand_pool, "morton", mask)], axis=0)

    return call(
        "far",
        functools.partial(far_kernel, lanes, grand_span),
        jax.ShapeDtypeStruct(leaf_dens.shape, BF16),
        [
            pltpu.VMEM((classes_count * own, lanes.total), BF16),
            pltpu.VMEM((classes_count * group, width), BF16),
            tiled(own * rhs_count, width),
        ],
        counts,
        grand_counts,
        inner_rows,
        range_rows,
        outer_rows,
        grand_pool,
        far_ops,
        down_ops,
    )


def solution(mesh):
    placed = (
        P(("morton", "sub"), None, None),
        P(("morton", "sub"), None),
        P(("morton", "sub"), None),
        P("morton", None),
        P("morton", None),
        P(),
        P(),
        P(),
    )
    return jax.shard_map(
        shards,
        mesh=mesh,
        in_specs=placed,
        out_specs=P(("morton", "sub"), None, None),
        check_vma=False,
    )
```

```python
import functools

import jax
import jax.numpy as jnp
from jax import lax
from jax.experimental import pallas as pl
from jax.experimental.pallas import tpu as pltpu
from jax.sharding import PartitionSpec as P

LANES = 128
F32 = jnp.float32
BF16 = jnp.bfloat16


def swapped(value, axis, mask):
    count = lax.axis_size(axis)
    return lax.ppermute(value, axis, [(i, i ^ mask) for i in range(count)])


def masks_of(count):
    return [1 << bit for bit in range(count.bit_length() - 1)]


class Lanes:
    def __init__(self, rhs_count, width):
        self.rhs_count, self.width = rhs_count, width
        self.main = width // LANES * LANES
        self.tail = width - self.main
        self.per_tile = LANES // self.tail if self.tail else 1
        self.tail_tiles = -(-rhs_count // self.per_tile) if self.tail else 0
        self.total = rhs_count * self.main + self.tail_tiles * LANES

    def main_of(self, n):
        return slice(n * self.main, (n + 1) * self.main)

    def tail_of(self, n):
        start = self.rhs_count * self.main + n // self.per_tile * LANES
        start += n % self.per_tile * self.tail
        return slice(start, start + self.tail)

    def take(self, rows, n):
        return jnp.concatenate([rows[:, self.main_of(n)], rows[:, self.tail_of(n)]], axis=1)


def tiles_of(width):
    return -(-width // LANES)


def fill(scratch, rows):
    for tile in range(scratch.shape[0]):
        part = rows[:, tile * LANES : (tile + 1) * LANES]
        scratch[tile, :, : part.shape[1]] = part


def every(scratch, start, size, stride, width):
    parts = [scratch[tile, pl.ds(start, size, stride=stride), :] for tile in range(tiles_of(width))]
    parts[-1] = parts[-1][:, : width - (len(parts) - 1) * LANES]
    return jnp.concatenate(parts, axis=1)


def flat_kernel(lanes, dens_ref, out_ref, wide):
    own, rhs_count, width = dens_ref.shape
    fill(wide, dens_ref[...].astype(F32).reshape(own * rhs_count, width))
    tails = []
    for n in range(rhs_count):
        rows = every(wide, n, own, rhs_count, width).astype(BF16)
        out_ref[:, lanes.main_of(n)] = rows[:, : lanes.main]
        tails.append(rows[:, lanes.main :])
    for tile in range(lanes.tail_tiles):
        parts = tails[tile * lanes.per_tile : (tile + 1) * lanes.per_tile]
        spare = LANES - len(parts) * lanes.tail
        parts.append(jnp.zeros((own, spare), BF16))
        start = rhs_count * lanes.main + tile * LANES
        out_ref[:, start : start + LANES] = jnp.concatenate(parts, axis=1)


def hot_rows(values, count):
    rows = lax.broadcasted_iota(jnp.int32, (count, values.shape[1]), 0)
    return jnp.where(rows == values, 1.0, 0.0).astype(BF16)


def class_counts(classes, sources, classes_count, pool_size):
    return lax.dot_general(
        hot_rows(classes, classes_count),
        hot_rows(sources, pool_size),
        (((1,), (1,)), ((), ())),
        preferred_element_type=F32,
    )


def counts_kernel(
    rhs_count,
    span,
    sources_ref,
    classes_ref,
    grand_sources_ref,
    grand_classes_ref,
    _up_ref,
    _far_ref,
    _down_ref,
    counts_ref,
    grand_counts_ref,
    wide,
):
    own = sources_ref.shape[0]
    pool_size = counts_ref.shape[1]
    classes_count = counts_ref.shape[0] // own
    range_size = pool_size // 3
    half = range_size // own // 2
    sub_index, morton_index = lax.axis_index("sub"), lax.axis_index("morton")
    odd = morton_index % 2
    row_pick = sub_index // span
    grand_index = morton_index * grand_sources_ref.shape[0] + row_pick
    for t in range(own):
        sources = sources_ref[t : t + 1, :]
        slot = sources // range_size
        inside = sources - slot * range_size
        slot = jnp.where(odd == 1, slot, 2 - slot)
        inside = inside ^ (sub_index * own)
        block = inside // own
        inside += (block % 2 * half + block // 2 - block) * own
        places = slot * range_size + inside
        counts = class_counts(
            classes_ref[t : t + 1, :], places, classes_count, wide.shape[0] * LANES
        )
        for tile in range(wide.shape[0]):
            part = counts[:, tile * LANES : (tile + 1) * LANES]
            wide[tile, pl.ds(t, classes_count, stride=own), :] = part
    counts_ref[...] = every(wide, 0, own * classes_count, 1, pool_size).astype(BF16)
    group = grand_counts_ref.shape[0] // classes_count
    spread = grand_counts_ref.shape[1]
    places = grand_sources_ref[pl.ds(row_pick, 1), :] ^ grand_index
    classes = grand_classes_ref[pl.ds(row_pick, 1), :]
    entries = places.shape[1]
    column_grand = lax.broadcasted_iota(jnp.int32, (spread, entries), 0) // rhs_count
    source_hot = jnp.where(column_grand == places, 1.0, 0.0).astype(BF16)
    row_class = lax.broadcasted_iota(jnp.int32, (classes_count * group, entries), 0) // group
    class_hot = jnp.where(row_class == classes, 1.0, 0.0).astype(BF16)
    all_pairs = lax.dot_general(
        class_hot, source_hot, (((1,), (1,)), ((), ())), preferred_element_type=F32
    )
    row_rhs = lax.broadcasted_iota(jnp.int32, all_pairs.shape, 0) % group
    column_rhs = lax.broadcasted_iota(jnp.int32, all_pairs.shape, 1) % rhs_count
    grand_counts_ref[...] = jnp.where(row_rhs == column_rhs, all_pairs, 0.0).astype(BF16)


def grand_kernel(lanes, span, rows_ref, up_ref, out_ref, wide, parents):
    rhs_count, width = lanes.rhs_count, lanes.width
    range_size = rows_ref.shape[0]
    fan = up_ref.shape[0]
    parent_count = range_size // fan
    position = lax.axis_index("sub") % span
    fill(wide, rows_ref[...].astype(F32))
    total = jnp.zeros((rhs_count * parent_count, width), F32)
    for k in range(fan):
        rows = every(wide, k, parent_count, fan, lanes.total)
        left = jnp.concatenate([lanes.take(rows, n) for n in range(rhs_count)], axis=0)
        total += jnp.dot(left.astype(BF16), up_ref[k], preferred_element_type=F32)
    fill(parents, total.astype(BF16).astype(F32))
    per_block = fan // span
    half = parent_count // per_block // 2
    for grand in range(parent_count // fan):
        total = jnp.zeros((rhs_count, width), F32)
        for child in range(fan):
            block = grand * span + child // per_block
            held = (block % 2 * half + block // 2) * per_block + child % per_block
            rows = every(parents, held, rhs_count, parent_count, width)
            operator = ((child // per_block) ^ position) * per_block + child % per_block
            total += jnp.dot(rows.astype(BF16), up_ref[operator], preferred_element_type=F32)
        out_ref[grand * rhs_count : (grand + 1) * rhs_count, :] = total.astype(BF16)


def far_kernel(
    lanes,
    span,
    counts_ref,
    grand_counts_ref,
    inner_ref,
    range_ref,
    outer_even_ref,
    outer_odd_ref,
    grand_pool_ref,
    far_ref,
    down_ref,
    out_ref,
    aggregate,
    grand_aggregate,
    far_rows,
):
    own, rhs_count, width = out_ref.shape
    classes_count = far_ref.shape[0]
    fan = down_ref.shape[0]
    group = grand_counts_ref.shape[0] // classes_count
    parents_here = own // fan
    position = lax.axis_index("sub") % span
    grand_aggregate[...] = jnp.dot(
        grand_counts_ref[...], grand_pool_ref[...], preferred_element_type=F32
    ).astype(BF16)
    refs = (inner_ref, range_ref, outer_even_ref, outer_odd_ref)
    pool = jnp.concatenate([ref[...] for ref in refs], axis=0)
    aggregate[...] = jnp.dot(counts_ref[...], pool, preferred_element_type=F32).astype(BF16)
    total = jnp.zeros((rhs_count * own + group, width), F32)
    for c in range(classes_count):
        rows = aggregate[c * own : (c + 1) * own, :]
        parts = [lanes.take(rows, n) for n in range(rhs_count)]
        parts.append(grand_aggregate[c * group : (c + 1) * group, :])
        total += jnp.dot(jnp.concatenate(parts, axis=0), far_ref[c], preferred_element_type=F32)
    pad = jnp.zeros((own, far_rows.shape[0] * LANES - width), F32)
    for n in range(rhs_count):
        rows = jnp.concatenate([total[n * own : (n + 1) * own, :], pad], axis=1)
        for tile in range(far_rows.shape[0]):
            part = rows[:, tile * LANES : (tile + 1) * LANES]
            far_rows[tile, pl.ds(n, own, stride=rhs_count), :] = part
    grand_local = total[rhs_count * own :, :].astype(BF16)
    parent_local = []
    for j in range(parents_here):
        operator = down_ref[position * parents_here + j]
        local = jnp.dot(grand_local, operator, preferred_element_type=F32)
        parent_local.append(local[:rhs_count, :])
    parent_local = jnp.concatenate(parent_local, axis=0).astype(BF16)
    for k in range(fan):
        downward = jnp.dot(parent_local, down_ref[k], preferred_element_type=F32)
        for j in range(parents_here):
            leaf = j * fan + k
            local = every(far_rows, leaf * rhs_count, rhs_count, 1, width)
            local += downward[j * rhs_count : (j + 1) * rhs_count, :]
            out_ref[leaf] = local.astype(BF16)


def tiled(rows, width):
    return pltpu.VMEM((tiles_of(width), rows, LANES), F32)


def call(kernel, outs, scratch, *operands):
    whole = pl.BlockSpec(memory_space=pltpu.VMEM)
    operands = [pltpu.with_memory_space_constraint(x, pltpu.VMEM) for x in operands]
    return pl.pallas_call(
        kernel,
        out_shape=outs,
        in_specs=[whole] * len(operands),
        out_specs=jax.tree.map(lambda _: whole, outs),
        scratch_shapes=scratch,
        compiler_params=pltpu.CompilerParams(vmem_limit_bytes=16 << 20),
    )(*operands)


def shards(
    leaf_dens, leaf_sources, leaf_classes, grand_sources, grand_classes, up_ops, far_ops, down_ops
):
    own, rhs_count, width = leaf_dens.shape
    classes_count = far_ops.shape[0]
    fan = up_ops.shape[0]
    sub_count, morton_count = lax.axis_size("sub"), lax.axis_size("morton")
    range_size = own * sub_count
    leaves_of_grand = fan * fan
    grand_span = leaves_of_grand // own
    grands_here = range_size // leaves_of_grand
    grand_count = morton_count * grands_here
    lanes = Lanes(rhs_count, width)
    struct = pltpu.VMEM

    rows = call(
        functools.partial(flat_kernel, lanes),
        struct((own, lanes.total), BF16),
        [tiled(own * rhs_count, width)],
        leaf_dens,
    )
    held = {0: rows}
    for mask in reversed(masks_of(sub_count)[1:]):
        order = sorted(held)
        joined = jnp.concatenate([held[p] for p in order], axis=0)
        other = swapped(joined, "sub", mask)
        for at, p in enumerate(order):
            held[p ^ mask] = other[at * own : (at + 1) * own]
    even_rows = jnp.concatenate([held[p] for p in sorted(held)], axis=0)
    odd_rows = swapped(even_rows, "sub", 1)
    pairs = [(i, i + 1) for i in range(1, morton_count - 1, 2)]
    outer_even = lax.ppermute(even_rows, "morton", pairs + [(j, i) for i, j in pairs])
    outer_odd = swapped(outer_even, "sub", 1)
    range_rows = jnp.concatenate([even_rows, odd_rows], axis=0)
    inner_rows = swapped(range_rows, "morton", 1)

    group = -(-rhs_count // 16) * 16
    counts, grand_counts = call(
        functools.partial(counts_kernel, rhs_count, grand_span),
        (
            struct((classes_count * own, 3 * range_size), BF16),
            struct((classes_count * group, grand_count * rhs_count), BF16),
        ),
        [tiled(classes_count * own, 3 * range_size)],
        leaf_sources,
        leaf_classes,
        grand_sources,
        grand_classes,
        up_ops,
        far_ops,
        down_ops,
    )

    grand_pool = call(
        functools.partial(grand_kernel, lanes, grand_span),
        struct((grands_here * rhs_count, width), BF16),
        [
            tiled(range_size, lanes.total),
            tiled(rhs_count * range_size // fan, width),
        ],
        range_rows,
        up_ops,
    )
    for mask in masks_of(morton_count):
        other = swapped(grand_pool, "morton", mask)
        grand_pool = jnp.concatenate([grand_pool, other], axis=0)

    return call(
        functools.partial(far_kernel, lanes, grand_span),
        jax.ShapeDtypeStruct(leaf_dens.shape, BF16),
        [
            pltpu.VMEM((classes_count * own, lanes.total), BF16),
            pltpu.VMEM((classes_count * group, width), BF16),
            tiled(own * rhs_count, width),
        ],
        counts,
        grand_counts,
        inner_rows,
        range_rows,
        outer_even,
        outer_odd,
        grand_pool,
        far_ops,
        down_ops,
    )


def solution(mesh):
    placed = (
        P(("morton", "sub"), None, None),
        P(("morton", "sub"), None),
        P(("morton", "sub"), None),
        P("morton", None),
        P("morton", None),
        P(),
        P(),
        P(),
    )
    return jax.shard_map(
        shards,
        mesh=mesh,
        in_specs=placed,
        out_specs=P(("morton", "sub"), None, None),
        check_vma=False,
    )
```

```python
import functools

import jax
import jax.numpy as jnp
from jax import lax
from jax.experimental import pallas as pl
from jax.experimental.pallas import tpu as pltpu
from jax.sharding import PartitionSpec as P

LANES = 128
F32 = jnp.float32
BF16 = jnp.bfloat16


def swapped(value, axis, mask):
    count = lax.axis_size(axis)
    return lax.ppermute(value, axis, [(i, i ^ mask) for i in range(count)])


def masks_of(count):
    return [1 << bit for bit in range(count.bit_length() - 1)]


class Lanes:
    def __init__(self, rhs_count, width):
        self.rhs_count, self.width = rhs_count, width
        self.main = width // LANES * LANES
        self.tail = width - self.main
        self.per_tile = LANES // self.tail if self.tail else 1
        self.tail_tiles = -(-rhs_count // self.per_tile) if self.tail else 0
        self.total = rhs_count * self.main + self.tail_tiles * LANES

    def main_of(self, n):
        return slice(n * self.main, (n + 1) * self.main)

    def tail_of(self, n):
        start = self.rhs_count * self.main + n // self.per_tile * LANES
        start += n % self.per_tile * self.tail
        return slice(start, start + self.tail)

    def take(self, rows, n):
        return jnp.concatenate([rows[:, self.main_of(n)], rows[:, self.tail_of(n)]], axis=1)


def tiles_of(width):
    return -(-width // LANES)


def fill(scratch, rows):
    for tile in range(scratch.shape[0]):
        part = rows[:, tile * LANES : (tile + 1) * LANES]
        scratch[tile, :, : part.shape[1]] = part


def every(scratch, start, size, stride, width):
    parts = [scratch[tile, pl.ds(start, size, stride=stride), :] for tile in range(tiles_of(width))]
    parts[-1] = parts[-1][:, : width - (len(parts) - 1) * LANES]
    return jnp.concatenate(parts, axis=1)


def flat_kernel(lanes, dens_ref, out_ref, wide):
    own, rhs_count, width = dens_ref.shape
    fill(wide, dens_ref[...].astype(F32).reshape(own * rhs_count, width))
    tails = []
    for n in range(rhs_count):
        rows = every(wide, n, own, rhs_count, width).astype(BF16)
        out_ref[:, lanes.main_of(n)] = rows[:, : lanes.main]
        tails.append(rows[:, lanes.main :])
    for tile in range(lanes.tail_tiles):
        parts = tails[tile * lanes.per_tile : (tile + 1) * lanes.per_tile]
        spare = LANES - len(parts) * lanes.tail
        parts.append(jnp.zeros((own, spare), BF16))
        start = rhs_count * lanes.main + tile * LANES
        out_ref[:, start : start + LANES] = jnp.concatenate(parts, axis=1)


def hot_rows(values, count):
    rows = lax.broadcasted_iota(jnp.int32, (count, values.shape[1]), 0)
    return jnp.where(rows == values, 1.0, 0.0).astype(BF16)


def class_counts(classes, sources, classes_count, pool_size):
    return lax.dot_general(
        hot_rows(classes, classes_count),
        hot_rows(sources, pool_size),
        (((1,), (1,)), ((), ())),
        preferred_element_type=F32,
    )


def counts_kernel(
    rhs_count,
    span,
    sources_ref,
    classes_ref,
    grand_sources_ref,
    grand_classes_ref,
    _up_ref,
    counts_ref,
    grand_counts_ref,
    wide,
):
    own = sources_ref.shape[0]
    pool_size = counts_ref.shape[1]
    classes_count = counts_ref.shape[0] // own
    range_size = pool_size // 3
    half = range_size // own // 2
    sub_index, morton_index = lax.axis_index("sub"), lax.axis_index("morton")
    odd = morton_index % 2
    row_pick = sub_index // span
    grand_index = morton_index * grand_sources_ref.shape[0] + row_pick
    for t in range(own):
        sources = sources_ref[t : t + 1, :]
        slot = sources // range_size
        inside = sources - slot * range_size
        slot = jnp.where(odd == 1, slot, 2 - slot)
        inside = inside ^ (sub_index * own)
        block = inside // own
        inside += (block % 2 * half + block // 2 - block) * own
        places = slot * range_size + inside
        counts = class_counts(
            classes_ref[t : t + 1, :], places, classes_count, wide.shape[0] * LANES
        )
        for tile in range(wide.shape[0]):
            part = counts[:, tile * LANES : (tile + 1) * LANES]
            wide[tile, pl.ds(t, classes_count, stride=own), :] = part
    counts_ref[...] = every(wide, 0, own * classes_count, 1, pool_size).astype(BF16)
    group = grand_counts_ref.shape[0] // classes_count
    spread = grand_counts_ref.shape[1]
    places = grand_sources_ref[pl.ds(row_pick, 1), :] ^ grand_index
    classes = grand_classes_ref[pl.ds(row_pick, 1), :]
    entries = places.shape[1]
    column_grand = lax.broadcasted_iota(jnp.int32, (spread, entries), 0) // rhs_count
    source_hot = jnp.where(column_grand == places, 1.0, 0.0).astype(BF16)
    row_class = lax.broadcasted_iota(jnp.int32, (classes_count * group, entries), 0) // group
    class_hot = jnp.where(row_class == classes, 1.0, 0.0).astype(BF16)
    all_pairs = lax.dot_general(
        class_hot, source_hot, (((1,), (1,)), ((), ())), preferred_element_type=F32
    )
    row_rhs = lax.broadcasted_iota(jnp.int32, all_pairs.shape, 0) % group
    column_rhs = lax.broadcasted_iota(jnp.int32, all_pairs.shape, 1) % rhs_count
    grand_counts_ref[...] = jnp.where(row_rhs == column_rhs, all_pairs, 0.0).astype(BF16)


def grand_kernel(lanes, span, rows_ref, up_ref, out_ref, wide, parents):
    rhs_count, width = lanes.rhs_count, lanes.width
    range_size = rows_ref.shape[0]
    fan = up_ref.shape[0]
    parent_count = range_size // fan
    position = lax.axis_index("sub") % span
    fill(wide, rows_ref[...].astype(F32))
    total = jnp.zeros((rhs_count * parent_count, width), F32)
    for k in range(fan):
        rows = every(wide, k, parent_count, fan, lanes.total)
        left = jnp.concatenate([lanes.take(rows, n) for n in range(rhs_count)], axis=0)
        total += jnp.dot(left.astype(BF16), up_ref[k], preferred_element_type=F32)
    fill(parents, total.astype(BF16).astype(F32))
    per_block = fan // span
    half = parent_count // per_block // 2
    for grand in range(parent_count // fan):
        total = jnp.zeros((rhs_count, width), F32)
        for child in range(fan):
            block = grand * span + child // per_block
            held = (block % 2 * half + block // 2) * per_block + child % per_block
            rows = every(parents, held, rhs_count, parent_count, width)
            operator = ((child // per_block) ^ position) * per_block + child % per_block
            total += jnp.dot(rows.astype(BF16), up_ref[operator], preferred_element_type=F32)
        out_ref[grand * rhs_count : (grand + 1) * rhs_count, :] = total.astype(BF16)


def far_kernel(
    lanes,
    span,
    counts_ref,
    grand_counts_ref,
    inner_ref,
    range_ref,
    outer_even_ref,
    outer_odd_ref,
    grand_pool_ref,
    far_ref,
    down_ref,
    _ready_ref,
    out_ref,
    aggregate,
    grand_aggregate,
    far_rows,
):
    own, rhs_count, width = out_ref.shape
    classes_count = far_ref.shape[0]
    fan = down_ref.shape[0]
    group = grand_counts_ref.shape[0] // classes_count
    parents_here = own // fan
    position = lax.axis_index("sub") % span
    grand_aggregate[...] = jnp.dot(
        grand_counts_ref[...], grand_pool_ref[...], preferred_element_type=F32
    ).astype(BF16)
    refs = (inner_ref, range_ref, outer_even_ref, outer_odd_ref)
    pool = jnp.concatenate([ref[...] for ref in refs], axis=0)
    aggregate[...] = jnp.dot(counts_ref[...], pool, preferred_element_type=F32).astype(BF16)
    total = jnp.zeros((rhs_count * own + group, width), F32)
    for c in range(classes_count):
        rows = aggregate[c * own : (c + 1) * own, :]
        parts = [lanes.take(rows, n) for n in range(rhs_count)]
        parts.append(grand_aggregate[c * group : (c + 1) * group, :])
        total += jnp.dot(jnp.concatenate(parts, axis=0), far_ref[c], preferred_element_type=F32)
    pad = jnp.zeros((own, far_rows.shape[0] * LANES - width), F32)
    for n in range(rhs_count):
        rows = jnp.concatenate([total[n * own : (n + 1) * own, :], pad], axis=1)
        for tile in range(far_rows.shape[0]):
            part = rows[:, tile * LANES : (tile + 1) * LANES]
            far_rows[tile, pl.ds(n, own, stride=rhs_count), :] = part
    grand_local = total[rhs_count * own :, :].astype(BF16)
    parent_local = []
    for j in range(parents_here):
        operator = down_ref[position * parents_here + j]
        local = jnp.dot(grand_local, operator, preferred_element_type=F32)
        parent_local.append(local[:rhs_count, :])
    parent_local = jnp.concatenate(parent_local, axis=0).astype(BF16)
    for k in range(fan):
        downward = jnp.dot(parent_local, down_ref[k], preferred_element_type=F32)
        for j in range(parents_here):
            leaf = j * fan + k
            local = every(far_rows, leaf * rhs_count, rhs_count, 1, width)
            local += downward[j * rhs_count : (j + 1) * rhs_count, :]
            out_ref[leaf] = local.astype(BF16)


def ready_kernel(_far_ref, _down_ref, out_ref):
    out_ref[...] = jnp.zeros(out_ref.shape, F32)


def tiled(rows, width):
    return pltpu.VMEM((tiles_of(width), rows, LANES), F32)


def call(kernel, outs, scratch, *operands):
    whole = pl.BlockSpec(memory_space=pltpu.VMEM)
    operands = [pltpu.with_memory_space_constraint(x, pltpu.VMEM) for x in operands]
    return pl.pallas_call(
        kernel,
        out_shape=outs,
        in_specs=[whole] * len(operands),
        out_specs=jax.tree.map(lambda _: whole, outs),
        scratch_shapes=scratch,
        compiler_params=pltpu.CompilerParams(vmem_limit_bytes=16 << 20),
    )(*operands)


def shards(
    leaf_dens, leaf_sources, leaf_classes, grand_sources, grand_classes, up_ops, far_ops, down_ops
):
    own, rhs_count, width = leaf_dens.shape
    classes_count = far_ops.shape[0]
    fan = up_ops.shape[0]
    sub_count, morton_count = lax.axis_size("sub"), lax.axis_size("morton")
    range_size = own * sub_count
    leaves_of_grand = fan * fan
    grand_span = leaves_of_grand // own
    grands_here = range_size // leaves_of_grand
    grand_count = morton_count * grands_here
    lanes = Lanes(rhs_count, width)
    struct = pltpu.VMEM

    rows = call(
        functools.partial(flat_kernel, lanes),
        struct((own, lanes.total), BF16),
        [tiled(own * rhs_count, width)],
        leaf_dens,
    )
    held = {0: rows}
    for mask in reversed(masks_of(sub_count)[1:]):
        order = sorted(held)
        joined = jnp.concatenate([held[p] for p in order], axis=0)
        other = swapped(joined, "sub", mask)
        for at, p in enumerate(order):
            held[p ^ mask] = other[at * own : (at + 1) * own]
    even_rows = jnp.concatenate([held[p] for p in sorted(held)], axis=0)
    odd_rows = swapped(even_rows, "sub", 1)
    pairs = [(i, i + 1) for i in range(1, morton_count - 1, 2)]
    outer_even = lax.ppermute(even_rows, "morton", pairs + [(j, i) for i, j in pairs])
    outer_odd = swapped(outer_even, "sub", 1)
    range_rows = jnp.concatenate([even_rows, odd_rows], axis=0)
    inner_rows = swapped(range_rows, "morton", 1)

    group = -(-rhs_count // 16) * 16
    counts, grand_counts = call(
        functools.partial(counts_kernel, rhs_count, grand_span),
        (
            struct((classes_count * own, 3 * range_size), BF16),
            struct((classes_count * group, grand_count * rhs_count), BF16),
        ),
        [tiled(classes_count * own, 3 * range_size)],
        leaf_sources,
        leaf_classes,
        grand_sources,
        grand_classes,
        up_ops,
    )
    ready = call(ready_kernel, struct((8, LANES), F32), [], far_ops, down_ops)

    grand_pool = call(
        functools.partial(grand_kernel, lanes, grand_span),
        struct((grands_here * rhs_count, width), BF16),
        [
            tiled(range_size, lanes.total),
            tiled(rhs_count * range_size // fan, width),
        ],
        range_rows,
        up_ops,
    )
    for mask in masks_of(morton_count):
        other = swapped(grand_pool, "morton", mask)
        grand_pool = jnp.concatenate([grand_pool, other], axis=0)

    return call(
        functools.partial(far_kernel, lanes, grand_span),
        jax.ShapeDtypeStruct(leaf_dens.shape, BF16),
        [
            pltpu.VMEM((classes_count * own, lanes.total), BF16),
            pltpu.VMEM((classes_count * group, width), BF16),
            tiled(own * rhs_count, width),
        ],
        counts,
        grand_counts,
        inner_rows,
        range_rows,
        outer_even,
        outer_odd,
        grand_pool,
        far_ops,
        down_ops,
        ready,
    )


def solution(mesh):
    placed = (
        P(("morton", "sub"), None, None),
        P(("morton", "sub"), None),
        P(("morton", "sub"), None),
        P("morton", None),
        P("morton", None),
        P(),
        P(),
        P(),
    )
    return jax.shard_map(
        shards,
        mesh=mesh,
        in_specs=placed,
        out_specs=P(("morton", "sub"), None, None),
        check_vma=False,
    )
```

```python
import functools

import jax
import jax.numpy as jnp
from jax import lax
from jax.experimental import pallas as pl
from jax.experimental.pallas import tpu as pltpu
from jax.sharding import PartitionSpec as P

LANES = 128
F32 = jnp.float32
BF16 = jnp.bfloat16


def swapped(value, axis, mask):
    count = lax.axis_size(axis)
    return lax.ppermute(value, axis, [(i, i ^ mask) for i in range(count)])


def masks_of(count):
    return [1 << bit for bit in range(count.bit_length() - 1)]


class Lanes:
    def __init__(self, rhs_count, width):
        self.rhs_count, self.width = rhs_count, width
        self.main = width // LANES * LANES
        self.tail = width - self.main
        self.per_tile = LANES // self.tail if self.tail else 1
        self.tail_tiles = -(-rhs_count // self.per_tile) if self.tail else 0
        self.total = rhs_count * self.main + self.tail_tiles * LANES

    def main_of(self, n):
        return slice(n * self.main, (n + 1) * self.main)

    def tail_of(self, n):
        start = self.rhs_count * self.main + n // self.per_tile * LANES
        start += n % self.per_tile * self.tail
        return slice(start, start + self.tail)

    def take(self, rows, n):
        return jnp.concatenate([rows[:, self.main_of(n)], rows[:, self.tail_of(n)]], axis=1)


def tiles_of(width):
    return -(-width // LANES)


def fill(scratch, rows):
    for tile in range(scratch.shape[0]):
        part = rows[:, tile * LANES : (tile + 1) * LANES]
        scratch[tile, :, : part.shape[1]] = part


def every(scratch, start, size, stride, width):
    parts = [scratch[tile, pl.ds(start, size, stride=stride), :] for tile in range(tiles_of(width))]
    parts[-1] = parts[-1][:, : width - (len(parts) - 1) * LANES]
    return jnp.concatenate(parts, axis=1)


def flat_kernel(lanes, dens_ref, out_ref, wide):
    own, rhs_count, width = dens_ref.shape
    fill(wide, dens_ref[...].astype(F32).reshape(own * rhs_count, width))
    tails = []
    for n in range(rhs_count):
        rows = every(wide, n, own, rhs_count, width).astype(BF16)
        out_ref[:, lanes.main_of(n)] = rows[:, : lanes.main]
        tails.append(rows[:, lanes.main :])
    for tile in range(lanes.tail_tiles):
        parts = tails[tile * lanes.per_tile : (tile + 1) * lanes.per_tile]
        spare = LANES - len(parts) * lanes.tail
        parts.append(jnp.zeros((own, spare), BF16))
        start = rhs_count * lanes.main + tile * LANES
        out_ref[:, start : start + LANES] = jnp.concatenate(parts, axis=1)


def hot_rows(values, count):
    rows = lax.broadcasted_iota(jnp.int32, (count, values.shape[1]), 0)
    return jnp.where(rows == values, 1.0, 0.0).astype(BF16)


def class_counts(classes, sources, classes_count, pool_size):
    return lax.dot_general(
        hot_rows(classes, classes_count),
        hot_rows(sources, pool_size),
        (((1,), (1,)), ((), ())),
        preferred_element_type=F32,
    )


def counts_kernel(
    rhs_count,
    span,
    sources_ref,
    classes_ref,
    grand_sources_ref,
    grand_classes_ref,
    _up_ref,
    counts_ref,
    grand_counts_ref,
    wide,
):
    own = sources_ref.shape[0]
    pool_size = counts_ref.shape[1]
    classes_count = counts_ref.shape[0] // own
    range_size = pool_size // 3
    half = range_size // own // 2
    sub_index, morton_index = lax.axis_index("sub"), lax.axis_index("morton")
    odd = morton_index % 2
    row_pick = sub_index // span
    grand_index = morton_index * grand_sources_ref.shape[0] + row_pick
    for t in range(own):
        sources = sources_ref[t : t + 1, :]
        slot = sources // range_size
        inside = sources - slot * range_size
        slot = jnp.where(odd == 1, slot, 2 - slot)
        inside = inside ^ (sub_index * own)
        block = inside // own
        inside += (block % 2 * half + block // 2 - block) * own
        places = slot * range_size + inside
        counts = class_counts(
            classes_ref[t : t + 1, :], places, classes_count, wide.shape[0] * LANES
        )
        for tile in range(wide.shape[0]):
            part = counts[:, tile * LANES : (tile + 1) * LANES]
            wide[tile, pl.ds(t, classes_count, stride=own), :] = part
    counts_ref[...] = every(wide, 0, own * classes_count, 1, pool_size).astype(BF16)
    group = grand_counts_ref.shape[0] // classes_count
    spread = grand_counts_ref.shape[1]
    places = grand_sources_ref[pl.ds(row_pick, 1), :] ^ grand_index
    classes = grand_classes_ref[pl.ds(row_pick, 1), :]
    entries = places.shape[1]
    column_grand = lax.broadcasted_iota(jnp.int32, (spread, entries), 0) // rhs_count
    source_hot = jnp.where(column_grand == places, 1.0, 0.0).astype(BF16)
    row_class = lax.broadcasted_iota(jnp.int32, (classes_count * group, entries), 0) // group
    class_hot = jnp.where(row_class == classes, 1.0, 0.0).astype(BF16)
    all_pairs = lax.dot_general(
        class_hot, source_hot, (((1,), (1,)), ((), ())), preferred_element_type=F32
    )
    row_rhs = lax.broadcasted_iota(jnp.int32, all_pairs.shape, 0) % group
    column_rhs = lax.broadcasted_iota(jnp.int32, all_pairs.shape, 1) % rhs_count
    grand_counts_ref[...] = jnp.where(row_rhs == column_rhs, all_pairs, 0.0).astype(BF16)


def grand_kernel(lanes, span, rows_ref, up_ref, out_ref, wide, parents):
    rhs_count, width = lanes.rhs_count, lanes.width
    range_size = rows_ref.shape[0]
    fan = up_ref.shape[0]
    parent_count = range_size // fan
    position = lax.axis_index("sub") % span
    fill(wide, rows_ref[...].astype(F32))
    total = jnp.zeros((rhs_count * parent_count, width), F32)
    for k in range(fan):
        rows = every(wide, k, parent_count, fan, lanes.total)
        left = jnp.concatenate([lanes.take(rows, n) for n in range(rhs_count)], axis=0)
        total += jnp.dot(left.astype(BF16), up_ref[k], preferred_element_type=F32)
    fill(parents, total.astype(BF16).astype(F32))
    per_block = fan // span
    half = parent_count // per_block // 2
    for grand in range(parent_count // fan):
        total = jnp.zeros((rhs_count, width), F32)
        for child in range(fan):
            block = grand * span + child // per_block
            held = (block % 2 * half + block // 2) * per_block + child % per_block
            rows = every(parents, held, rhs_count, parent_count, width)
            operator = ((child // per_block) ^ position) * per_block + child % per_block
            total += jnp.dot(rows.astype(BF16), up_ref[operator], preferred_element_type=F32)
        out_ref[grand * rhs_count : (grand + 1) * rhs_count, :] = total.astype(BF16)


def far_kernel(
    lanes,
    span,
    counts_ref,
    grand_counts_ref,
    inner_ref,
    range_ref,
    outer_even_ref,
    outer_odd_ref,
    grand_pool_ref,
    far_ref,
    down_ref,
    _ready_ref,
    out_ref,
    aggregate,
    grand_aggregate,
    far_rows,
):
    own, rhs_count, width = out_ref.shape
    classes_count = far_ref.shape[0]
    fan = down_ref.shape[0]
    group = grand_counts_ref.shape[0] // classes_count
    parents_here = own // fan
    position = lax.axis_index("sub") % span
    grand_aggregate[...] = jnp.dot(
        grand_counts_ref[...], grand_pool_ref[...], preferred_element_type=F32
    ).astype(BF16)
    refs = (inner_ref, range_ref, outer_even_ref, outer_odd_ref)
    pool = jnp.concatenate([ref[...] for ref in refs], axis=0)
    aggregate[...] = jnp.dot(counts_ref[...], pool, preferred_element_type=F32).astype(BF16)
    total = jnp.zeros((rhs_count * own + group, width), F32)
    for c in range(classes_count):
        rows = aggregate[c * own : (c + 1) * own, :]
        parts = [lanes.take(rows, n) for n in range(rhs_count)]
        parts.append(grand_aggregate[c * group : (c + 1) * group, :])
        total += jnp.dot(jnp.concatenate(parts, axis=0), far_ref[c], preferred_element_type=F32)
    pad = jnp.zeros((own, far_rows.shape[0] * LANES - width), F32)
    for n in range(rhs_count):
        rows = jnp.concatenate([total[n * own : (n + 1) * own, :], pad], axis=1)
        for tile in range(far_rows.shape[0]):
            part = rows[:, tile * LANES : (tile + 1) * LANES]
            far_rows[tile, pl.ds(n, own, stride=rhs_count), :] = part
    grand_local = total[rhs_count * own :, :].astype(BF16)
    parent_local = []
    for j in range(parents_here):
        operator = down_ref[position * parents_here + j]
        local = jnp.dot(grand_local, operator, preferred_element_type=F32)
        parent_local.append(local[:rhs_count, :])
    parent_local = jnp.concatenate(parent_local, axis=0).astype(BF16)
    for k in range(fan):
        downward = jnp.dot(parent_local, down_ref[k], preferred_element_type=F32)
        for j in range(parents_here):
            leaf = j * fan + k
            local = every(far_rows, leaf * rhs_count, rhs_count, 1, width)
            local += downward[j * rhs_count : (j + 1) * rhs_count, :]
            out_ref[leaf] = local.astype(BF16)


def ready_kernel(_far_ref, _down_ref, out_ref):
    out_ref[...] = jnp.zeros(out_ref.shape, F32)


def tiled(rows, width):
    return pltpu.VMEM((tiles_of(width), rows, LANES), F32)


def call(kernel, outs, scratch, *operands):
    whole = pl.BlockSpec(memory_space=pltpu.VMEM)
    operands = [pltpu.with_memory_space_constraint(x, pltpu.VMEM) for x in operands]
    return pl.pallas_call(
        kernel,
        out_shape=outs,
        in_specs=[whole] * len(operands),
        out_specs=jax.tree.map(lambda _: whole, outs),
        scratch_shapes=scratch,
        compiler_params=pltpu.CompilerParams(vmem_limit_bytes=16 << 20),
    )(*operands)


def shards(
    leaf_dens, leaf_sources, leaf_classes, grand_sources, grand_classes, up_ops, far_ops, down_ops
):
    own, rhs_count, width = leaf_dens.shape
    classes_count = far_ops.shape[0]
    fan = up_ops.shape[0]
    sub_count, morton_count = lax.axis_size("sub"), lax.axis_size("morton")
    range_size = own * sub_count
    leaves_of_grand = fan * fan
    grand_span = leaves_of_grand // own
    grands_here = range_size // leaves_of_grand
    grand_count = morton_count * grands_here
    lanes = Lanes(rhs_count, width)
    struct = pltpu.VMEM

    rows = call(
        functools.partial(flat_kernel, lanes),
        struct((own, lanes.total), BF16),
        [tiled(own * rhs_count, width)],
        leaf_dens,
    )
    held = {0: rows}
    for mask in reversed(masks_of(sub_count)[1:]):
        order = sorted(held)
        joined = jnp.concatenate([held[p] for p in order], axis=0)
        other = swapped(joined, "sub", mask)
        for at, p in enumerate(order):
            held[p ^ mask] = other[at * own : (at + 1) * own]
    near_own = swapped(rows, "sub", 1)
    rest_rows = jnp.concatenate([held[p] for p in sorted(held) if p], axis=0)
    even_rows = jnp.concatenate([rows, rest_rows], axis=0)
    odd_rows = jnp.concatenate([near_own, swapped(rest_rows, "sub", 1)], axis=0)
    pairs = [(i, i + 1) for i in range(1, morton_count - 1, 2)]
    ends = [(0, morton_count - 1), (morton_count - 1, 0)]
    swaps = pairs + [(j, i) for i, j in pairs] + ends
    outer_even = lax.ppermute(even_rows, "morton", swaps)
    outer_odd = swapped(outer_even, "sub", 1)
    range_rows = jnp.concatenate([even_rows, odd_rows], axis=0)
    inner_rows = swapped(range_rows, "morton", 1)

    group = -(-rhs_count // 16) * 16
    counts, grand_counts = call(
        functools.partial(counts_kernel, rhs_count, grand_span),
        (
            struct((classes_count * own, 3 * range_size), BF16),
            struct((classes_count * group, grand_count * rhs_count), BF16),
        ),
        [tiled(classes_count * own, 3 * range_size)],
        leaf_sources,
        leaf_classes,
        grand_sources,
        grand_classes,
        up_ops,
    )
    ready = call(ready_kernel, struct((8, LANES), F32), [], far_ops, down_ops)

    grand_pool = call(
        functools.partial(grand_kernel, lanes, grand_span),
        struct((grands_here * rhs_count, width), BF16),
        [
            tiled(range_size, lanes.total),
            tiled(rhs_count * range_size // fan, width),
        ],
        range_rows,
        up_ops,
    )
    for mask in masks_of(morton_count):
        other = swapped(grand_pool, "morton", mask)
        grand_pool = jnp.concatenate([grand_pool, other], axis=0)

    return call(
        functools.partial(far_kernel, lanes, grand_span),
        jax.ShapeDtypeStruct(leaf_dens.shape, BF16),
        [
            pltpu.VMEM((classes_count * own, lanes.total), BF16),
            pltpu.VMEM((classes_count * group, width), BF16),
            tiled(own * rhs_count, width),
        ],
        counts,
        grand_counts,
        inner_rows,
        range_rows,
        outer_even,
        outer_odd,
        grand_pool,
        far_ops,
        down_ops,
        ready,
    )


def solution(mesh):
    placed = (
        P(("morton", "sub"), None, None),
        P(("morton", "sub"), None),
        P(("morton", "sub"), None),
        P("morton", None),
        P("morton", None),
        P(),
        P(),
        P(),
    )
    return jax.shard_map(
        shards,
        mesh=mesh,
        in_specs=placed,
        out_specs=P(("morton", "sub"), None, None),
        check_vma=False,
    )
```

```python
import functools

import jax
import jax.numpy as jnp
from jax import lax
from jax.experimental import pallas as pl
from jax.experimental.pallas import tpu as pltpu
from jax.sharding import PartitionSpec as P

LANES = 128
F32 = jnp.float32
BF16 = jnp.bfloat16


def swapped(value, axis, mask):
    count = lax.axis_size(axis)
    return lax.ppermute(value, axis, [(i, i ^ mask) for i in range(count)])


def masks_of(count):
    return [1 << bit for bit in range(count.bit_length() - 1)]


class Lanes:
    def __init__(self, rhs_count, width):
        self.rhs_count, self.width = rhs_count, width
        self.main = width // LANES * LANES
        self.tail = width - self.main
        self.per_tile = LANES // self.tail if self.tail else 1
        self.tail_tiles = -(-rhs_count // self.per_tile) if self.tail else 0
        self.total = rhs_count * self.main + self.tail_tiles * LANES

    def main_of(self, n):
        return slice(n * self.main, (n + 1) * self.main)

    def tail_of(self, n):
        start = self.rhs_count * self.main + n // self.per_tile * LANES
        start += n % self.per_tile * self.tail
        return slice(start, start + self.tail)

    def take(self, rows, n):
        return jnp.concatenate([rows[:, self.main_of(n)], rows[:, self.tail_of(n)]], axis=1)


def tiles_of(width):
    return -(-width // LANES)


def fill(scratch, rows):
    for tile in range(scratch.shape[0]):
        part = rows[:, tile * LANES : (tile + 1) * LANES]
        scratch[tile, :, : part.shape[1]] = part


def every(scratch, start, size, stride, width):
    parts = [scratch[tile, pl.ds(start, size, stride=stride), :] for tile in range(tiles_of(width))]
    parts[-1] = parts[-1][:, : width - (len(parts) - 1) * LANES]
    return jnp.concatenate(parts, axis=1)


def flat_kernel(lanes, dens_ref, out_ref, wide):
    own, rhs_count, width = dens_ref.shape
    fill(wide, dens_ref[...].astype(F32).reshape(own * rhs_count, width))
    tails = []
    for n in range(rhs_count):
        rows = every(wide, n, own, rhs_count, width).astype(BF16)
        out_ref[:, lanes.main_of(n)] = rows[:, : lanes.main]
        tails.append(rows[:, lanes.main :])
    for tile in range(lanes.tail_tiles):
        parts = tails[tile * lanes.per_tile : (tile + 1) * lanes.per_tile]
        spare = LANES - len(parts) * lanes.tail
        parts.append(jnp.zeros((own, spare), BF16))
        start = rhs_count * lanes.main + tile * LANES
        out_ref[:, start : start + LANES] = jnp.concatenate(parts, axis=1)


def hot_rows(values, count):
    rows = lax.broadcasted_iota(jnp.int32, (count, values.shape[1]), 0)
    return jnp.where(rows == values, 1.0, 0.0).astype(BF16)


def class_counts(classes, sources, classes_count, pool_size):
    return lax.dot_general(
        hot_rows(classes, classes_count),
        hot_rows(sources, pool_size),
        (((1,), (1,)), ((), ())),
        preferred_element_type=F32,
    )


def counts_kernel(
    rhs_count,
    span,
    sources_ref,
    classes_ref,
    grand_sources_ref,
    grand_classes_ref,
    _up_ref,
    counts_ref,
    grand_counts_ref,
    wide,
):
    own = sources_ref.shape[0]
    pool_size = counts_ref.shape[1]
    classes_count = counts_ref.shape[0] // own
    range_size = pool_size // 3
    half = range_size // own // 2
    sub_index, morton_index = lax.axis_index("sub"), lax.axis_index("morton")
    odd = morton_index % 2
    row_pick = sub_index // span
    grand_index = morton_index * grand_sources_ref.shape[0] + row_pick
    for t in range(own):
        sources = sources_ref[t : t + 1, :]
        slot = sources // range_size
        inside = sources - slot * range_size
        slot = jnp.where(odd == 1, slot, 2 - slot)
        inside = inside ^ (sub_index * own)
        block = inside // own
        inside += (block % 2 * half + block // 2 - block) * own
        places = slot * range_size + inside
        counts = class_counts(
            classes_ref[t : t + 1, :], places, classes_count, wide.shape[0] * LANES
        )
        for tile in range(wide.shape[0]):
            part = counts[:, tile * LANES : (tile + 1) * LANES]
            wide[tile, pl.ds(t, classes_count, stride=own), :] = part
    counts_ref[...] = every(wide, 0, own * classes_count, 1, pool_size).astype(BF16)
    group = grand_counts_ref.shape[0] // classes_count
    spread = grand_counts_ref.shape[1]
    places = grand_sources_ref[pl.ds(row_pick, 1), :] ^ grand_index
    classes = grand_classes_ref[pl.ds(row_pick, 1), :]
    entries = places.shape[1]
    column_grand = lax.broadcasted_iota(jnp.int32, (spread, entries), 0) // rhs_count
    source_hot = jnp.where(column_grand == places, 1.0, 0.0).astype(BF16)
    row_class = lax.broadcasted_iota(jnp.int32, (classes_count * group, entries), 0) // group
    class_hot = jnp.where(row_class == classes, 1.0, 0.0).astype(BF16)
    all_pairs = lax.dot_general(
        class_hot, source_hot, (((1,), (1,)), ((), ())), preferred_element_type=F32
    )
    row_rhs = lax.broadcasted_iota(jnp.int32, all_pairs.shape, 0) % group
    column_rhs = lax.broadcasted_iota(jnp.int32, all_pairs.shape, 1) % rhs_count
    grand_counts_ref[...] = jnp.where(row_rhs == column_rhs, all_pairs, 0.0).astype(BF16)


def grand_kernel(lanes, span, rows_ref, up_ref, out_ref, wide, parents):
    rhs_count, width = lanes.rhs_count, lanes.width
    range_size = rows_ref.shape[0]
    fan = up_ref.shape[0]
    parent_count = range_size // fan
    position = lax.axis_index("sub") % span
    fill(wide, rows_ref[...].astype(F32))
    total = jnp.zeros((rhs_count * parent_count, width), F32)
    for k in range(fan):
        rows = every(wide, k, parent_count, fan, lanes.total)
        left = jnp.concatenate([lanes.take(rows, n) for n in range(rhs_count)], axis=0)
        total += jnp.dot(left.astype(BF16), up_ref[k], preferred_element_type=F32)
    fill(parents, total.astype(BF16).astype(F32))
    per_block = fan // span
    half = parent_count // per_block // 2
    for grand in range(parent_count // fan):
        total = jnp.zeros((rhs_count, width), F32)
        for child in range(fan):
            block = grand * span + child // per_block
            held = (block % 2 * half + block // 2) * per_block + child % per_block
            rows = every(parents, held, rhs_count, parent_count, width)
            operator = ((child // per_block) ^ position) * per_block + child % per_block
            total += jnp.dot(rows.astype(BF16), up_ref[operator], preferred_element_type=F32)
        out_ref[grand * rhs_count : (grand + 1) * rhs_count, :] = total.astype(BF16)


def far_kernel(
    lanes,
    span,
    counts_ref,
    grand_counts_ref,
    inner_ref,
    range_ref,
    outer_even_ref,
    outer_odd_ref,
    grand_pool_ref,
    far_ref,
    down_ref,
    tails_ref,
    out_ref,
    aggregate,
    grand_aggregate,
    far_rows,
):
    own, rhs_count, width = out_ref.shape
    classes_count = far_ref.shape[0]
    fan = down_ref.shape[0]
    group = grand_counts_ref.shape[0] // classes_count
    parents_here = own // fan
    position = lax.axis_index("sub") % span
    grand_aggregate[...] = jnp.dot(
        grand_counts_ref[...], grand_pool_ref[...], preferred_element_type=F32
    ).astype(BF16)
    refs = (inner_ref, range_ref, outer_even_ref, outer_odd_ref)
    pool = jnp.concatenate([ref[...] for ref in refs], axis=0)
    aggregate[...] = jnp.dot(counts_ref[...], pool, preferred_element_type=F32).astype(BF16)
    main, step = lanes.main, tails_ref.shape[0] // classes_count
    spare = jnp.zeros((own, step - lanes.tail), BF16)
    spare_grand = jnp.zeros((group, step - lanes.tail), BF16)
    lefts = []
    for n in range(rhs_count):
        parts = []
        for c in range(classes_count):
            parts += [aggregate[c * own : (c + 1) * own, lanes.tail_of(n)], spare]
        lefts.append(jnp.concatenate(parts, axis=1))
    parts = []
    for c in range(classes_count):
        parts += [grand_aggregate[c * group : (c + 1) * group, main:], spare_grand]
    lefts.append(jnp.concatenate(parts, axis=1))
    total = jnp.dot(jnp.concatenate(lefts, axis=0), tails_ref[...], preferred_element_type=F32)
    for first in range(0, classes_count, 4):
        lefts = []
        for c in range(first, first + 4):
            rows = aggregate[c * own : (c + 1) * own, :]
            parts = [rows[:, lanes.main_of(n)] for n in range(rhs_count)]
            parts.append(grand_aggregate[c * group : (c + 1) * group, :main])
            lefts.append(jnp.concatenate(parts, axis=0))
        right = far_ref[first : first + 4, :main, :].reshape(4 * main, width)
        total += jnp.dot(jnp.concatenate(lefts, axis=1), right, preferred_element_type=F32)
    pad = jnp.zeros((own, far_rows.shape[0] * LANES - width), F32)
    for n in range(rhs_count):
        rows = jnp.concatenate([total[n * own : (n + 1) * own, :], pad], axis=1)
        for tile in range(far_rows.shape[0]):
            part = rows[:, tile * LANES : (tile + 1) * LANES]
            far_rows[tile, pl.ds(n, own, stride=rhs_count), :] = part
    grand_local = total[rhs_count * own :, :].astype(BF16)
    parent_local = []
    for j in range(parents_here):
        operator = down_ref[position * parents_here + j]
        local = jnp.dot(grand_local, operator, preferred_element_type=F32)
        parent_local.append(local[:rhs_count, :])
    parent_local = jnp.concatenate(parent_local, axis=0).astype(BF16)
    for k in range(fan):
        downward = jnp.dot(parent_local, down_ref[k], preferred_element_type=F32)
        for j in range(parents_here):
            leaf = j * fan + k
            local = every(far_rows, leaf * rhs_count, rhs_count, 1, width)
            local += downward[j * rhs_count : (j + 1) * rhs_count, :]
            out_ref[leaf] = local.astype(BF16)


def tails_kernel(main, far_ref, _down_ref, out_ref, wide):
    classes_count, width = far_ref.shape[0], far_ref.shape[2]
    tail = far_ref.shape[1] - main
    step = out_ref.shape[0] // classes_count
    for c in range(classes_count):
        wide[c * step : c * step + tail, :] = far_ref[c, main:, :].astype(F32)
        wide[c * step + tail : (c + 1) * step, :] = jnp.zeros((step - tail, width), F32)
    out_ref[...] = wide[...].astype(BF16)


def tiled(rows, width):
    return pltpu.VMEM((tiles_of(width), rows, LANES), F32)


def call(kernel, outs, scratch, *operands):
    whole = pl.BlockSpec(memory_space=pltpu.VMEM)
    operands = [pltpu.with_memory_space_constraint(x, pltpu.VMEM) for x in operands]
    return pl.pallas_call(
        kernel,
        out_shape=outs,
        in_specs=[whole] * len(operands),
        out_specs=jax.tree.map(lambda _: whole, outs),
        scratch_shapes=scratch,
        compiler_params=pltpu.CompilerParams(vmem_limit_bytes=16 << 20),
    )(*operands)


def shards(
    leaf_dens, leaf_sources, leaf_classes, grand_sources, grand_classes, up_ops, far_ops, down_ops
):
    own, rhs_count, width = leaf_dens.shape
    classes_count = far_ops.shape[0]
    fan = up_ops.shape[0]
    sub_count, morton_count = lax.axis_size("sub"), lax.axis_size("morton")
    range_size = own * sub_count
    leaves_of_grand = fan * fan
    grand_span = leaves_of_grand // own
    grands_here = range_size // leaves_of_grand
    grand_count = morton_count * grands_here
    lanes = Lanes(rhs_count, width)
    struct = pltpu.VMEM

    rows = call(
        functools.partial(flat_kernel, lanes),
        struct((own, lanes.total), BF16),
        [tiled(own * rhs_count, width)],
        leaf_dens,
    )
    held = {0: rows}
    for mask in reversed(masks_of(sub_count)[1:]):
        order = sorted(held)
        joined = jnp.concatenate([held[p] for p in order], axis=0)
        other = swapped(joined, "sub", mask)
        for at, p in enumerate(order):
            held[p ^ mask] = other[at * own : (at + 1) * own]
    near_own = swapped(rows, "sub", 1)
    rest_rows = jnp.concatenate([held[p] for p in sorted(held) if p], axis=0)
    even_rows = jnp.concatenate([rows, rest_rows], axis=0)
    odd_rows = jnp.concatenate([near_own, swapped(rest_rows, "sub", 1)], axis=0)
    pairs = [(i, i + 1) for i in range(1, morton_count - 1, 2)]
    ends = [(0, morton_count - 1), (morton_count - 1, 0)]
    swaps = pairs + [(j, i) for i, j in pairs] + ends
    outer_even = lax.ppermute(even_rows, "morton", swaps)
    outer_odd = swapped(outer_even, "sub", 1)
    range_rows = jnp.concatenate([even_rows, odd_rows], axis=0)
    inner_rows = swapped(range_rows, "morton", 1)

    group = -(-rhs_count // 16) * 16
    counts, grand_counts = call(
        functools.partial(counts_kernel, rhs_count, grand_span),
        (
            struct((classes_count * own, 3 * range_size), BF16),
            struct((classes_count * group, grand_count * rhs_count), BF16),
        ),
        [tiled(classes_count * own, 3 * range_size)],
        leaf_sources,
        leaf_classes,
        grand_sources,
        grand_classes,
        up_ops,
    )
    tail_step = -(-lanes.tail // 8) * 8
    tails = call(
        functools.partial(tails_kernel, lanes.main),
        struct((classes_count * tail_step, width), BF16),
        [pltpu.VMEM((classes_count * tail_step, width), F32)],
        far_ops,
        down_ops,
    )

    grand_pool = call(
        functools.partial(grand_kernel, lanes, grand_span),
        struct((grands_here * rhs_count, width), BF16),
        [
            tiled(range_size, lanes.total),
            tiled(rhs_count * range_size // fan, width),
        ],
        range_rows,
        up_ops,
    )
    for mask in masks_of(morton_count):
        other = swapped(grand_pool, "morton", mask)
        grand_pool = jnp.concatenate([grand_pool, other], axis=0)

    return call(
        functools.partial(far_kernel, lanes, grand_span),
        jax.ShapeDtypeStruct(leaf_dens.shape, BF16),
        [
            pltpu.VMEM((classes_count * own, lanes.total), BF16),
            pltpu.VMEM((classes_count * group, width), BF16),
            tiled(own * rhs_count, width),
        ],
        counts,
        grand_counts,
        inner_rows,
        range_rows,
        outer_even,
        outer_odd,
        grand_pool,
        far_ops,
        down_ops,
        tails,
    )


def solution(mesh):
    placed = (
        P(("morton", "sub"), None, None),
        P(("morton", "sub"), None),
        P(("morton", "sub"), None),
        P("morton", None),
        P("morton", None),
        P(),
        P(),
        P(),
    )
    return jax.shard_map(
        shards,
        mesh=mesh,
        in_specs=placed,
        out_specs=P(("morton", "sub"), None, None),
        check_vma=False,
    )
```

```python
import functools

import jax
import jax.numpy as jnp
from jax import lax
from jax.experimental import pallas as pl
from jax.experimental.pallas import tpu as pltpu
from jax.sharding import PartitionSpec as P

LANES = 128
F32 = jnp.float32
BF16 = jnp.bfloat16


def swapped(value, axis, mask):
    count = lax.axis_size(axis)
    return lax.ppermute(value, axis, [(i, i ^ mask) for i in range(count)])


def masks_of(count):
    return [1 << bit for bit in range(count.bit_length() - 1)]


class Lanes:
    def __init__(self, rhs_count, width):
        self.rhs_count, self.width = rhs_count, width
        self.main = width // LANES * LANES
        self.tail = width - self.main
        self.per_tile = LANES // self.tail if self.tail else 1
        self.tail_tiles = -(-rhs_count // self.per_tile) if self.tail else 0
        self.total = rhs_count * self.main + self.tail_tiles * LANES

    def main_of(self, n):
        return slice(n * self.main, (n + 1) * self.main)

    def tail_of(self, n):
        start = self.rhs_count * self.main + n // self.per_tile * LANES
        start += n % self.per_tile * self.tail
        return slice(start, start + self.tail)

    def take(self, rows, n):
        return jnp.concatenate([rows[:, self.main_of(n)], rows[:, self.tail_of(n)]], axis=1)


def tiles_of(width):
    return -(-width // LANES)


def fill(scratch, rows):
    for tile in range(scratch.shape[0]):
        part = rows[:, tile * LANES : (tile + 1) * LANES]
        scratch[tile, :, : part.shape[1]] = part


def every(scratch, start, size, stride, width):
    parts = [scratch[tile, pl.ds(start, size, stride=stride), :] for tile in range(tiles_of(width))]
    parts[-1] = parts[-1][:, : width - (len(parts) - 1) * LANES]
    return jnp.concatenate(parts, axis=1)


def flat_kernel(lanes, dens_ref, out_ref, wide):
    own, rhs_count, width = dens_ref.shape
    fill(wide, dens_ref[...].astype(F32).reshape(own * rhs_count, width))
    tails = []
    for n in range(rhs_count):
        rows = every(wide, n, own, rhs_count, width).astype(BF16)
        out_ref[:, lanes.main_of(n)] = rows[:, : lanes.main]
        tails.append(rows[:, lanes.main :])
    for tile in range(lanes.tail_tiles):
        parts = tails[tile * lanes.per_tile : (tile + 1) * lanes.per_tile]
        spare = LANES - len(parts) * lanes.tail
        parts.append(jnp.zeros((own, spare), BF16))
        start = rhs_count * lanes.main + tile * LANES
        out_ref[:, start : start + LANES] = jnp.concatenate(parts, axis=1)


def hot_rows(values, count):
    rows = lax.broadcasted_iota(jnp.int32, (count, values.shape[1]), 0)
    return jnp.where(rows == values, 1.0, 0.0).astype(BF16)


def class_counts(classes, sources, classes_count, pool_size):
    return lax.dot_general(
        hot_rows(classes, classes_count),
        hot_rows(sources, pool_size),
        (((1,), (1,)), ((), ())),
        preferred_element_type=F32,
    )


def counts_kernel(
    rhs_count,
    span,
    sources_ref,
    classes_ref,
    grand_sources_ref,
    grand_classes_ref,
    _up_ref,
    counts_ref,
    grand_counts_ref,
    wide,
):
    own = sources_ref.shape[0]
    pool_size = counts_ref.shape[1]
    classes_count = counts_ref.shape[0] // own
    range_size = pool_size // 3
    half = range_size // own // 2
    sub_index, morton_index = lax.axis_index("sub"), lax.axis_index("morton")
    odd = morton_index % 2
    row_pick = sub_index // span
    grand_index = morton_index * grand_sources_ref.shape[0] + row_pick
    for t in range(own):
        sources = sources_ref[t : t + 1, :]
        slot = sources // range_size
        inside = sources - slot * range_size
        slot = jnp.where(odd == 1, slot, 2 - slot)
        inside = inside ^ (sub_index * own)
        block = inside // own
        inside += (block % 2 * half + block // 2 - block) * own
        places = slot * range_size + inside
        counts = class_counts(classes_ref[t : t + 1, :], places, classes_count, pool_size)
        spare = jnp.zeros((classes_count, wide.shape[0] * LANES - pool_size), F32)
        counts = jnp.concatenate([counts, spare], axis=1) if spare.size else counts
        for tile in range(wide.shape[0]):
            part = counts[:, tile * LANES : (tile + 1) * LANES]
            wide[tile, pl.ds(t, classes_count, stride=own), :] = part
    counts_ref[...] = every(wide, 0, own * classes_count, 1, pool_size).astype(BF16)
    group = grand_counts_ref.shape[0] // classes_count
    spread = grand_counts_ref.shape[1]
    places = grand_sources_ref[pl.ds(row_pick, 1), :] ^ grand_index
    classes = grand_classes_ref[pl.ds(row_pick, 1), :]
    entries = places.shape[1]
    column_grand = lax.broadcasted_iota(jnp.int32, (spread, entries), 0) // rhs_count
    source_hot = jnp.where(column_grand == places, 1.0, 0.0).astype(BF16)
    row_class = lax.broadcasted_iota(jnp.int32, (classes_count * group, entries), 0) // group
    class_hot = jnp.where(row_class == classes, 1.0, 0.0).astype(BF16)
    all_pairs = lax.dot_general(
        class_hot, source_hot, (((1,), (1,)), ((), ())), preferred_element_type=F32
    )
    row_rhs = lax.broadcasted_iota(jnp.int32, all_pairs.shape, 0) % group
    column_rhs = lax.broadcasted_iota(jnp.int32, all_pairs.shape, 1) % rhs_count
    grand_counts_ref[...] = jnp.where(row_rhs == column_rhs, all_pairs, 0.0).astype(BF16)


def grand_kernel(lanes, span, places, parts, *refs):
    rows_refs, up_ref, earlier = refs[:parts], refs[parts], refs[parts + 1 : -3]
    out_ref, wide, parents = refs[-3:]
    rhs_count, width = lanes.rhs_count, lanes.width
    fan = up_ref.shape[0]
    per_block = fan // span
    parent_count = wide.shape[1] // fan
    position = lax.axis_index("sub") % span
    start = 0
    for ref in rows_refs:
        rows = ref[...].astype(F32)
        for tile in range(wide.shape[0]):
            part = rows[:, tile * LANES : (tile + 1) * LANES]
            wide[tile, start : start + rows.shape[0], :] = part
        start += rows.shape[0]
    if start < wide.shape[1]:
        spare = jnp.zeros((wide.shape[1] - start, LANES), F32)
        for tile in range(wide.shape[0]):
            wide[tile, start:, :] = spare
    total = jnp.zeros((rhs_count * parent_count, width), F32)
    for k in range(fan):
        rows = every(wide, k, parent_count, fan, lanes.total)
        left = jnp.concatenate([lanes.take(rows, n) for n in range(rhs_count)], axis=0)
        total += jnp.dot(left.astype(BF16), up_ref[k], preferred_element_type=F32)
    fill(parents, total.astype(BF16).astype(F32))
    for grand in range(out_ref.shape[0] // rhs_count):
        held = slice(grand * rhs_count, (grand + 1) * rhs_count)
        total = earlier[0][held, :] if earlier else jnp.zeros((rhs_count, width), F32)
        for block, place in enumerate(places):
            if place // span != grand:
                continue
            for j in range(per_block):
                rows = every(parents, block * per_block + j, rhs_count, parent_count, width)
                operator = ((place % span) ^ position) * per_block + j
                total += jnp.dot(rows.astype(BF16), up_ref[operator], preferred_element_type=F32)
        out_ref[held, :] = total.astype(out_ref.dtype)


def far_kernel(
    lanes,
    span,
    counts_ref,
    grand_counts_ref,
    inner_ref,
    range_ref,
    outer_even_ref,
    outer_odd_ref,
    grand_pool_ref,
    far_ref,
    down_ref,
    tails_ref,
    out_ref,
    aggregate,
    grand_aggregate,
    far_rows,
):
    own, rhs_count, width = out_ref.shape
    classes_count = far_ref.shape[0]
    fan = down_ref.shape[0]
    group = grand_counts_ref.shape[0] // classes_count
    parents_here = own // fan
    position = lax.axis_index("sub") % span
    grand_aggregate[...] = jnp.dot(
        grand_counts_ref[...], grand_pool_ref[...], preferred_element_type=F32
    ).astype(BF16)
    refs = (inner_ref, range_ref, outer_even_ref, outer_odd_ref)
    pool = jnp.concatenate([ref[...] for ref in refs], axis=0)
    aggregate[...] = jnp.dot(counts_ref[...], pool, preferred_element_type=F32).astype(BF16)
    main, step = lanes.main, tails_ref.shape[0] // classes_count
    spare = jnp.zeros((own, step - lanes.tail), BF16)
    spare_grand = jnp.zeros((group, step - lanes.tail), BF16)
    lefts = []
    for n in range(rhs_count):
        parts = []
        for c in range(classes_count):
            parts += [aggregate[c * own : (c + 1) * own, lanes.tail_of(n)], spare]
        lefts.append(jnp.concatenate(parts, axis=1))
    parts = []
    for c in range(classes_count):
        parts += [grand_aggregate[c * group : (c + 1) * group, main:], spare_grand]
    lefts.append(jnp.concatenate(parts, axis=1))
    total = jnp.dot(jnp.concatenate(lefts, axis=0), tails_ref[...], preferred_element_type=F32)
    for first in range(0, classes_count, 4):
        lefts = []
        for c in range(first, first + 4):
            rows = aggregate[c * own : (c + 1) * own, :]
            parts = [rows[:, lanes.main_of(n)] for n in range(rhs_count)]
            parts.append(grand_aggregate[c * group : (c + 1) * group, :main])
            lefts.append(jnp.concatenate(parts, axis=0))
        right = far_ref[first : first + 4, :main, :].reshape(4 * main, width)
        total += jnp.dot(jnp.concatenate(lefts, axis=1), right, preferred_element_type=F32)
    pad = jnp.zeros((own, far_rows.shape[0] * LANES - width), F32)
    for n in range(rhs_count):
        rows = jnp.concatenate([total[n * own : (n + 1) * own, :], pad], axis=1)
        for tile in range(far_rows.shape[0]):
            part = rows[:, tile * LANES : (tile + 1) * LANES]
            far_rows[tile, pl.ds(n, own, stride=rhs_count), :] = part
    grand_local = total[rhs_count * own :, :].astype(BF16)
    parent_local = []
    for j in range(parents_here):
        operator = down_ref[position * parents_here + j]
        local = jnp.dot(grand_local, operator, preferred_element_type=F32)
        parent_local.append(local[:rhs_count, :])
    parent_local = jnp.concatenate(parent_local, axis=0).astype(BF16)
    for k in range(fan):
        downward = jnp.dot(parent_local, down_ref[k], preferred_element_type=F32)
        for j in range(parents_here):
            leaf = j * fan + k
            local = every(far_rows, leaf * rhs_count, rhs_count, 1, width)
            local += downward[j * rhs_count : (j + 1) * rhs_count, :]
            out_ref[leaf] = local.astype(BF16)


def tails_kernel(main, far_ref, _down_ref, out_ref, wide):
    classes_count, width = far_ref.shape[0], far_ref.shape[2]
    tail = far_ref.shape[1] - main
    step = out_ref.shape[0] // classes_count
    for c in range(classes_count):
        wide[c * step : c * step + tail, :] = far_ref[c, main:, :].astype(F32)
        wide[c * step + tail : (c + 1) * step, :] = jnp.zeros((step - tail, width), F32)
    out_ref[...] = wide[...].astype(BF16)


def tiled(rows, width):
    return pltpu.VMEM((tiles_of(width), rows, LANES), F32)


def call(kernel, outs, scratch, *operands):
    whole = pl.BlockSpec(memory_space=pltpu.VMEM)
    operands = [pltpu.with_memory_space_constraint(x, pltpu.VMEM) for x in operands]
    return pl.pallas_call(
        kernel,
        out_shape=outs,
        in_specs=[whole] * len(operands),
        out_specs=jax.tree.map(lambda _: whole, outs),
        scratch_shapes=scratch,
        compiler_params=pltpu.CompilerParams(vmem_limit_bytes=16 << 20),
    )(*operands)


def shards(
    leaf_dens, leaf_sources, leaf_classes, grand_sources, grand_classes, up_ops, far_ops, down_ops
):
    own, rhs_count, width = leaf_dens.shape
    classes_count = far_ops.shape[0]
    fan = up_ops.shape[0]
    sub_count, morton_count = lax.axis_size("sub"), lax.axis_size("morton")
    range_size = own * sub_count
    leaves_of_grand = fan * fan
    grand_span = leaves_of_grand // own
    grands_here = range_size // leaves_of_grand
    grand_count = morton_count * grands_here
    lanes = Lanes(rhs_count, width)
    struct = pltpu.VMEM

    rows = call(
        functools.partial(flat_kernel, lanes),
        struct((own, lanes.total), BF16),
        [tiled(own * rhs_count, width)],
        leaf_dens,
    )
    held = {0: rows}
    for mask in reversed(masks_of(sub_count)[1:]):
        order = sorted(held)
        joined = jnp.concatenate([held[p] for p in order], axis=0)
        other = swapped(joined, "sub", mask)
        for at, p in enumerate(order):
            held[p ^ mask] = other[at * own : (at + 1) * own]
    near_own = swapped(rows, "sub", 1)
    rest_rows = jnp.concatenate([held[p] for p in sorted(held) if p], axis=0)
    even_rows = jnp.concatenate([rows, rest_rows], axis=0)
    near_rest = swapped(rest_rows, "sub", 1)
    odd_rows = jnp.concatenate([near_own, near_rest], axis=0)
    pairs = [(i, i + 1) for i in range(1, morton_count - 1, 2)]
    ends = [(0, morton_count - 1), (morton_count - 1, 0)]
    swaps = pairs + [(j, i) for i, j in pairs] + ends
    outer_even = lax.ppermute(even_rows, "morton", swaps)
    outer_odd = swapped(outer_even, "sub", 1)
    range_rows = jnp.concatenate([even_rows, odd_rows], axis=0)
    inner_rows = swapped(range_rows, "morton", 1)

    group = rhs_count
    counts, grand_counts = call(
        functools.partial(counts_kernel, rhs_count, grand_span),
        (
            struct((classes_count * own, 3 * range_size), BF16),
            struct((classes_count * group, grand_count * rhs_count), BF16),
        ),
        [tiled(classes_count * own, 3 * range_size)],
        leaf_sources,
        leaf_classes,
        grand_sources,
        grand_classes,
        up_ops,
    )
    tail_step = -(-lanes.tail // 8) * 8
    tails = call(
        functools.partial(tails_kernel, lanes.main),
        struct((classes_count * tail_step, width), BF16),
        [pltpu.VMEM((classes_count * tail_step, width), F32)],
        far_ops,
        down_ops,
    )

    def grands(places, blocks, earlier, kind):
        parents = -(-len(places) * own // fan // 8) * 8
        return call(
            functools.partial(grand_kernel, lanes, grand_span, places, len(blocks)),
            struct((grands_here * rhs_count, width), kind),
            [tiled(parents * fan, lanes.total), tiled(rhs_count * parents, width)],
            *blocks,
            up_ops,
            *earlier,
        )

    evens, odds = list(range(0, sub_count, 2)), list(range(3, sub_count, 2))
    part = grands(evens + [1], [even_rows, near_own], [], F32)
    grand_pool = grands(odds, [near_rest], [part], BF16)
    for mask in masks_of(morton_count):
        other = swapped(grand_pool, "morton", mask)
        grand_pool = jnp.concatenate([grand_pool, other], axis=0)

    return call(
        functools.partial(far_kernel, lanes, grand_span),
        jax.ShapeDtypeStruct(leaf_dens.shape, BF16),
        [
            pltpu.VMEM((classes_count * own, lanes.total), BF16),
            pltpu.VMEM((classes_count * group, width), BF16),
            tiled(own * rhs_count, width),
        ],
        counts,
        grand_counts,
        inner_rows,
        range_rows,
        outer_even,
        outer_odd,
        grand_pool,
        far_ops,
        down_ops,
        tails,
    )


def solution(mesh):
    placed = (
        P(("morton", "sub"), None, None),
        P(("morton", "sub"), None),
        P(("morton", "sub"), None),
        P("morton", None),
        P("morton", None),
        P(),
        P(),
        P(),
    )
    return jax.shard_map(
        shards,
        mesh=mesh,
        in_specs=placed,
        out_specs=P(("morton", "sub"), None, None),
        check_vma=False,
    )
```
